128 devices in a mesh: grp: 4 (over y), seq: 32 (over x, z, core).
Axes of the slice: x: 4, y: 4, z: 4, core: 2. Of those that a mesh axis runs over, the one named last changes fastest.
Arguments:
- passage_q: bfloat16 [65536, 4096], P(('grp', 'seq')), may hold values from -8 to 8
- passage_k: bfloat16 [65536, 512], P(('grp', 'seq')), may hold values from -8 to 8
- passage_v: bfloat16 [65536, 512], P(('grp', 'seq')), may hold values from -6 to 6
- kept: int32 [128, 4], P(('grp', 'seq')), may hold values from 0 to 1, as said below
- context_map: int32 [4, 32], P('grp', 'seq'), may hold values from 0 to 127, as said below
- recompute_pos: int32 [4, 2048], P('grp', 'seq'), may hold values from 0 to 16383, as said below
- recompute_q: bfloat16 [4, 2048, 4096], P('grp', 'seq'), may hold values from -8 to 8
- recompute_k: bfloat16 [4, 2048, 512], P('grp', 'seq'), may hold values from -8 to 8
- recompute_v: bfloat16 [4, 2048, 512], P('grp', 'seq'), may hold values from -6 to 6
Outputs:
- passage_out: bfloat16 [65536, 4096], P(('grp', 'seq'))
- reader_out: bfloat16 [4, 2048, 4096], P('grp', 'seq')
The draws below stay inside these ranges and needn't reach their ends.
Inputs may be any that keep to these rules, and one draw needn't show every extreme that they name: Block 0 of every passage is kept; a passage keeps at most 3 of its 4 blocks, and some passage keeps exactly 3. `context_map`: every passage appears exactly once. Entry [g, s] names a passage encoded on a device whose seq index is s. `recompute_pos`: entries [g, s * 64] to [g, (s + 1) * 64 - 1] are distinct ascending positions from s * 512 to (s + 1) * 512 - 1.
All inputs are finite; a program needn't handle non-finite values.
Results may differ from the reference program's by a relative error of at most 0.005.
Values may be sent and summed in bfloat16 or wider, within the bound.
No kernel may reach another device: no remote copies, remote signals or barrier semaphores. Data moves between devices by JAX's collectives and lax.ppermute only.
A program may use at most 256 MiB of HBM per device.

```python
import jax
import jax.numpy as jnp
from jax import lax

HQ = 32
KVH = 4
HD = 128
PLEN = 512
BLK = 128
KEEP = 3
PASS_DEV = 1
NBLK = 4
NPASS = 128
CTX_LEN = 16384
R_DEV = 64
RECOMP = 2048
N_GRP = 4
N_SEQ = 32


def query_draw(key, salt, shape):
    subkey = jax.random.fold_in(key, salt)
    values = jnp.clip(jax.random.normal(subkey, shape, jnp.float32), -6.0, 6.0)
    return values.astype(jnp.bfloat16)


def key_draw(key, salt, shape):
    subkey = jax.random.fold_in(key, salt)
    values = jnp.clip(2.5 * jax.random.normal(subkey, shape, jnp.float32), -7.5, 7.5)
    return values.astype(jnp.bfloat16)


def draw_passage_q(key, part):
    return query_draw(key, 11, (NPASS * PLEN, HQ * HD))


def draw_passage_k(key, part):
    return key_draw(key, 21, (NPASS * PLEN, KVH * HD))


def draw_recompute_q(key, part):
    return query_draw(key, 31, (N_GRP, RECOMP, HQ * HD))


def draw_recompute_k(key, part):
    return key_draw(key, 41, (N_GRP, RECOMP, KVH * HD))


def draw_kept(key, part):
    extra = jax.random.randint(jax.random.fold_in(key, 51), (NPASS,), 0, KEEP)
    extra = extra.at[0].set(KEEP - 1)
    subkeys = jax.random.split(jax.random.fold_in(key, 52), NPASS)
    ranking = jax.vmap(lambda subkey: jax.random.permutation(subkey, NBLK - 1))(subkeys)
    others = (ranking < extra[:, None]).astype(jnp.int32)
    return jnp.concatenate([jnp.ones((NPASS, 1), jnp.int32), others], axis=1)


def draw_context_map(key, part):
    column_size = N_GRP * PASS_DEV
    subkeys = jax.random.split(jax.random.fold_in(key, 61), N_SEQ)
    orders = jax.vmap(lambda subkey: jax.random.permutation(subkey, column_size))(subkeys)
    chosen = orders.reshape(N_SEQ, N_GRP, PASS_DEV).transpose(1, 0, 2)
    source_group = chosen // PASS_DEV
    source_slot = chosen % PASS_DEV
    column_index = jnp.arange(N_SEQ).reshape(1, N_SEQ, 1)
    passage_ids = (source_group * N_SEQ + column_index) * PASS_DEV + source_slot
    return passage_ids.reshape(N_GRP, N_SEQ * PASS_DEV).astype(jnp.int32)


def draw_recompute_pos(key, part):
    span_rows = PASS_DEV * PLEN
    subkeys = jax.random.split(jax.random.fold_in(key, 71), N_GRP * N_SEQ)
    picked = jax.vmap(lambda subkey: jnp.sort(jax.random.permutation(subkey, span_rows)[:R_DEV]))(subkeys)
    starts = jnp.arange(N_GRP * N_SEQ) % N_SEQ * span_rows
    return (picked + starts[:, None]).reshape(N_GRP, RECOMP).astype(jnp.int32)


def levels(own_key, extent, pieces, low, high):
    level = 1.0
    for dim, parts in pieces:
        steps = jax.random.uniform(jax.random.fold_in(jax.random.fold_in(own_key, 6), dim), (parts,), jnp.float32, low / len(pieces), high / len(pieces))
        level = level * jnp.repeat(jnp.exp(steps), extent[dim] // parts).reshape((-1,) + (1,) * (len(extent) - 1 - dim))
    return level


def bell_draw(own_key, dims, width, reach, cuts=(), held_as=jnp.bfloat16):
    factor_of = levels(own_key, dims, cuts, -0.22, 0.18) if cuts else 1.0
    result = jax.random.normal(own_key, dims, jnp.float32) * width * factor_of
    return jnp.minimum(jnp.maximum(result, -reach), reach).astype(held_as)


def setup_inputs(seed: int = 0) -> dict:
    streams_of = jax.random.split(jax.random.key(seed), 10)
    passage_q = draw_passage_q(jax.random.fold_in(streams_of[9], 71), 0)
    passage_k = draw_passage_k(jax.random.fold_in(streams_of[9], 71), 0)
    passage_v = bell_draw(streams_of[2], (NPASS * PLEN, KVH * HD), 1.0, 6.0, ((0, 128),))
    kept = draw_kept(jax.random.fold_in(streams_of[9], 71), 0)
    context_map = draw_context_map(jax.random.fold_in(streams_of[9], 71), 0)
    recompute_pos = draw_recompute_pos(jax.random.fold_in(streams_of[9], 71), 0)
    recompute_q = draw_recompute_q(jax.random.fold_in(streams_of[9], 71), 0)
    recompute_k = draw_recompute_k(jax.random.fold_in(streams_of[9], 71), 0)
    recompute_v = bell_draw(streams_of[8], (N_GRP, RECOMP, KVH * HD), 1.0, 6.0, ((0, 4), (1, 32)))
    return {"passage_q": passage_q, "passage_k": passage_k, "passage_v": passage_v, "kept": kept, "context_map": context_map, "recompute_pos": recompute_pos, "recompute_q": recompute_q, "recompute_k": recompute_k, "recompute_v": recompute_v}


def passage_attention(queries, key_rows, value_rows):
    length = queries.shape[0]
    query_heads = queries.astype(jnp.float32).reshape(length, KVH, HQ // KVH, HD)
    key_heads = key_rows.astype(jnp.float32).reshape(length, KVH, HD)
    value_heads = value_rows.astype(jnp.float32).reshape(length, KVH, HD)
    scores = jnp.einsum('ikgd,jkd->kgij', query_heads, key_heads) * (HD ** -0.5)
    causal = jnp.arange(length)[:, None] >= jnp.arange(length)[None, :]
    scores = jnp.where(causal, scores, -jnp.inf)
    maximum = jnp.max(scores, axis=-1, keepdims=True)
    weights = jnp.exp(scores - maximum).astype(jnp.bfloat16)
    totals = jnp.sum(weights.astype(jnp.float32), axis=-1)
    mixture = jnp.einsum('kgij,jkd->ikgd', weights.astype(jnp.float32), value_heads)
    mixture = mixture / jnp.moveaxis(totals, -1, 0)[..., None]
    return mixture.reshape(length, HQ * HD).astype(jnp.bfloat16)


def encode_items(items):
    return passage_attention(items[0], items[1], items[2])


def reader_group(passage_k, passage_v, kept, slot_map, positions, queries, own_keys, own_values):
    context_keys = passage_k.reshape(NPASS, PLEN, KVH * HD)[slot_map].reshape(CTX_LEN, KVH, HD).astype(jnp.float32)
    context_values = passage_v.reshape(NPASS, PLEN, KVH * HD)[slot_map].reshape(CTX_LEN, KVH, HD).astype(jnp.float32)
    kept_rows = jnp.repeat(kept[slot_map], BLK, axis=1).reshape(CTX_LEN)
    key_pos = jnp.arange(CTX_LEN).astype(jnp.int32)
    query_block = 64
    block_total = RECOMP // query_block

    def attend(items):
        block_q, block_k, block_v, block_pos = items
        query_heads = block_q.astype(jnp.float32).reshape(query_block, KVH, HQ // KVH, HD)
        own_k = block_k.astype(jnp.float32).reshape(query_block, KVH, HD)
        own_v = block_v.astype(jnp.float32).reshape(query_block, KVH, HD)
        scores = jnp.einsum('rkgd,nkd->rkgn', query_heads, context_keys) * (HD ** -0.5)
        visible = (kept_rows[None, :] > 0) & (key_pos[None, :] < block_pos[:, None])
        scores = jnp.where(visible[:, None, None, :], scores, -jnp.inf)
        own_score = jnp.einsum('rkgd,rkd->rkg', query_heads, own_k) * (HD ** -0.5)
        maximum = jnp.maximum(jnp.max(scores, axis=-1), own_score)
        weights = jnp.exp(scores - maximum[..., None]).astype(jnp.bfloat16)
        own_weight = jnp.exp(own_score - maximum).astype(jnp.bfloat16).astype(jnp.float32)
        totals = jnp.sum(weights.astype(jnp.float32), axis=-1) + own_weight
        mixture = jnp.einsum('rkgn,nkd->rkgd', weights.astype(jnp.float32), context_values)
        mixture = mixture + own_weight[..., None] * own_v[:, :, None, :]
        return (mixture / totals[..., None]).reshape(query_block, HQ * HD).astype(jnp.bfloat16)

    items = (queries.reshape(block_total, query_block, HQ * HD), own_keys.reshape(block_total, query_block, KVH * HD), own_values.reshape(block_total, query_block, KVH * HD), positions.reshape(block_total, query_block))
    return lax.map(attend, items).reshape(RECOMP, HQ * HD)


def reference(passage_q, passage_k, passage_v, kept, context_map, recompute_pos, recompute_q, recompute_k, recompute_v):
    items = (passage_q.reshape(NPASS, PLEN, HQ * HD), passage_k.reshape(NPASS, PLEN, KVH * HD), passage_v.reshape(NPASS, PLEN, KVH * HD))
    passage_out = lax.map(encode_items, items).reshape(NPASS * PLEN, HQ * HD)
    groups = []
    for group_index in range(N_GRP):
        groups.append(reader_group(passage_k, passage_v, kept, context_map[group_index], recompute_pos[group_index], recompute_q[group_index], recompute_k[group_index], recompute_v[group_index]))
    reader_out = jnp.stack(groups)
    return passage_out, reader_out
```

```python
import functools
import math

import jax
import jax.numpy as jnp
from jax import lax
from jax.experimental import pallas as pl
from jax.experimental.pallas import tpu as pltpu
from jax.sharding import PartitionSpec as P

HQ = 32
KVH = 4
GQ = HQ // KVH
HD = 128
PLEN = 512
BLK = 128
KEEP = 3
NBLK = PLEN // BLK
R_DEV = 64
N_GRP = 4
N_X = 4
N_Z = 4
N_SEQ = 32
META = KEEP * BLK
PIECE = META + 16
KV2 = 2 * HD
QW = GQ * HD + 4 * HD
ROWS = GQ * R_DEV
EXP_SCALE = HD ** (-0.5) * math.log2(math.e)
FAR = 100
STEP = 4
STEPS = N_SEQ * KEEP // STEP
TAIL = KEEP + STEP - 1
PIECES = N_SEQ


NT = (((1,), (1,)), ((), ()))
bf16 = jnp.bfloat16
f32 = jnp.float32


def seq_of(x, z, c):
    return x * (N_Z * 2) + z * 2 + c


def shift_y(a, k):
    return lax.ppermute(a, "grp", [(i, (i + k) % N_GRP) for i in range(N_GRP)])


def seq_pairs(dx, dz, dc):
    return [
        (seq_of(x, z, c), seq_of((x + dx) % N_X, (z + dz) % N_Z, (c + dc) % 2))
        for x in range(N_X)
        for z in range(N_Z)
        for c in range(2)
    ]


def shift_seq(a, dx=0, dz=0, dc=0):
    return lax.ppermute(a, "seq", seq_pairs(dx, dz, dc))


def pack_kernel(s_ref, k_ref, v_ref, q_ref, rk_ref, rv_ref, pos_ref, a_ref, b_ref, q0, q1, q2, q3):
    kept = [s_ref[b] for b in range(NBLK)]
    before = [0]
    for b in range(NBLK):
        before.append(before[-1] + kept[b])
    count = before[NBLK]
    row = lax.broadcasted_iota(jnp.int32, (16, HD), 0)
    meta = jnp.where(row == 0, count, FAR)
    for j in range(KEEP):
        block = 0
        for b in range(NBLK):
            block = block + jnp.where((kept[b] > 0) & (before[b] == j), b, 0)
        number = jnp.where(j < count, block, FAR)
        meta = jnp.where(row == 1 + j, number, meta)
        start = pl.multiple_of(block * BLK, BLK)
        for h in range(KVH):
            out = a_ref if h < 2 else b_ref
            cols = slice(h * HD, (h + 1) * HD)
            rows = slice(j * BLK, (j + 1) * BLK)
            out[h % 2, rows, :HD] = k_ref[pl.ds(start, BLK), cols]
            out[h % 2, rows, HD:] = v_ref[pl.ds(start, BLK), cols]
    meta = meta.astype(f32).astype(bf16)
    for out in (a_ref, b_ref):
        for h in range(2):
            out[h, META:, :HD] = meta
            out[h, META:, HD:] = meta
    place = pos_ref[...]
    high = jnp.broadcast_to(place // 16, (R_DEV, HD)).astype(f32).astype(bf16)
    low = jnp.broadcast_to(place % 16, (R_DEV, HD)).astype(f32).astype(bf16)
    w = GQ * HD
    for d, out in enumerate((q0, q1, q2, q3)):
        h = lax.rem(s_ref[NBLK] + d, N_X)
        out[:, :w] = q_ref[:, pl.ds(pl.multiple_of(h * w, w), w)]
        cols = pl.ds(pl.multiple_of(h * HD, HD), HD)
        out[:, w : w + HD] = rk_ref[:, cols]
        out[:, w + HD : w + 2 * HD] = rv_ref[:, cols]
        out[:, w + 2 * HD : w + 3 * HD] = high
        out[:, w + 3 * HD :] = low


def pack(scalars, k, v, q, rk, rv, pos):
    half = jax.ShapeDtypeStruct((2, PIECE, KV2), bf16)
    query = jax.ShapeDtypeStruct((R_DEV, QW), bf16)
    vmem = pl.BlockSpec(memory_space=pltpu.VMEM)
    return pl.pallas_call(
        pack_kernel,
        out_shape=(half, half, query, query, query, query),
        in_specs=[pl.BlockSpec(memory_space=pltpu.SMEM)] + [vmem] * 6,
        out_specs=(vmem,) * 6,
        name="pack",
    )(scalars, k, v, q, rk, rv, pos)


def passage_kernel(q_ref, k_ref, v_ref, o_ref):
    ones = jnp.ones((PLEN, HD), bf16)
    values = jnp.concatenate([v_ref[...], ones], axis=1)
    keys = k_ref[...]
    row = lax.broadcasted_iota(jnp.int32, (BLK, BLK), 0)
    col = lax.broadcasted_iota(jnp.int32, (BLK, BLK), 1)
    hidden = jnp.concatenate([col > row] * GQ, axis=0)
    for i in range(NBLK):
        rows = slice(i * BLK, (i + 1) * BLK)
        n = (i + 1) * BLK
        q = jnp.concatenate([q_ref[rows, g * HD : (g + 1) * HD] for g in range(GQ)], axis=0)
        s = lax.dot_general(q, keys[:n], NT, preferred_element_type=f32)
        last = jnp.where(hidden, -jnp.inf, s[:, n - BLK :])
        s = last if i == 0 else jnp.concatenate([s[:, : n - BLK], last], axis=1)
        m = jnp.max(s, axis=1, keepdims=True)
        p = jnp.exp2((s - m) * EXP_SCALE).astype(bf16)
        mixed = jnp.dot(p, values[:n], preferred_element_type=f32)
        out = (mixed[:, :HD] / mixed[:, HD:]).astype(bf16)
        for g in range(GQ):
            o_ref[rows, g * HD : (g + 1) * HD] = out[g * BLK : (g + 1) * BLK]


def encode(q, k, v):
    w = GQ * HD
    return pl.pallas_call(
        passage_kernel,
        out_shape=jax.ShapeDtypeStruct((PLEN, HQ * HD), bf16),
        grid=(KVH,),
        in_specs=[
            pl.BlockSpec((PLEN, w), lambda h: (0, h)),
            pl.BlockSpec((PLEN, HD), lambda h: (0, h)),
            pl.BlockSpec((PLEN, HD), lambda h: (0, h)),
        ],
        out_specs=pl.BlockSpec((PLEN, w), lambda h: (0, h)),
        cost_estimate=pl.CostEstimate(
            flops=4 * PLEN * PLEN * HQ * HD, bytes_accessed=9 << 20, transcendentals=HQ * PLEN * PLEN
        ),
        name="encode",
    )(q, k, v)


def reader_kernel(s_ref, *refs):
    n_arr = PIECES // 2
    kv_in, q_in, outs = refs[:n_arr], refs[n_arr : n_arr + N_X], refs[n_arr + N_X : n_arr + 2 * N_X]
    kv, qs, scores, top, acc, table, starts, sems = refs[n_arr + 2 * N_X :]
    x, z, c = s_ref[0], s_ref[1], s_ref[2]
    copies = [pltpu.make_async_copy(q_in[d], qs.at[d], sems.at[d]) for d in range(N_X)]
    copies += [
        pltpu.make_async_copy(kv_in[a], kv.at[pl.ds(2 * a, 2)], sems.at[N_X + a]) for a in range(n_arr)
    ]
    for copy in copies:
        copy.start()
    for copy in copies:
        copy.wait()

    n = jnp.int32(0)
    for t in range(N_SEQ):
        tx, tz, tc = t // (N_Z * 2), (t // 2) % N_Z, t % 2
        piece = lax.rem(c + tc, 2) * 16 + lax.rem(tz - z + N_Z, N_Z) * 4 + lax.rem(x - tx + N_X, N_X)
        count = jnp.max(kv[piece, META : META + 1, :HD].astype(f32)).astype(jnp.int32)
        starts[t] = n
        for j in range(KEEP):
            table[n + j] = piece * KEEP + j
        n = n + count

    lane = lax.broadcasted_iota(jnp.int32, (1, BLK), 1)

    def block(code, cols):
        piece = code // KEEP
        first = pl.multiple_of(lax.rem(code, KEEP) * BLK, BLK)
        return kv[piece, pl.ds(first, BLK), cols]

    def visit(d, carry):
        shard = seq_of(lax.rem(x - d + N_X, N_X), z, c)
        w = GQ * HD
        q = jnp.concatenate([qs[d, :, g * HD : (g + 1) * HD] for g in range(GQ)], axis=0)
        own_k = jnp.concatenate([qs[d, :, w : w + HD]] * GQ, axis=0).astype(f32)
        own = jnp.sum(q.astype(f32) * own_k, axis=1, keepdims=True)
        total = starts[shard]
        full = total // STEP
        left = total - full * STEP

        codes = [jnp.where(u < left, table[full * STEP + u], d * KEEP) for u in range(STEP - 1)]
        codes += [d * KEEP + j for j in range(KEEP)]
        keys = jnp.concatenate([block(code, slice(0, HD)) for code in codes], axis=0)
        s = lax.dot_general(q, keys, NT, preferred_element_type=f32)
        place = qs[d, :, w + 2 * HD : w + 3 * HD].astype(f32) * 16 + qs[d, :, w + 3 * HD :].astype(f32)
        place = jnp.concatenate([place] * GQ, axis=0)
        lane_f = lane.astype(f32)
        best = jnp.broadcast_to(own, (ROWS, HD))
        for u in range(TAIL):
            part = s[:, u * BLK : (u + 1) * BLK]
            if u < STEP - 1:
                part = jnp.where(u < left, part, -jnp.inf)
            else:
                j = u - (STEP - 1)
                number = kv[d, META + 1 + j : META + 2 + j, :HD].astype(f32)
                part = jnp.where(number * BLK + lane_f < place, part, -jnp.inf)
            scores[STEPS + u // STEP, :, (u % STEP) * BLK : (u % STEP + 1) * BLK] = part
            best = jnp.maximum(best, part)
        top[...] = best

        def first_pass(g, carry):
            codes = [table[g * STEP + u] for u in range(STEP)]
            keys = jnp.concatenate([block(code, slice(0, HD)) for code in codes], axis=0)
            s = lax.dot_general(q, keys, NT, preferred_element_type=f32)
            scores[g] = s
            best = top[...]
            for u in range(STEP):
                best = jnp.maximum(best, s[:, u * BLK : (u + 1) * BLK])
            top[...] = best
            return carry

        lax.fori_loop(0, full, first_pass, 0)
        m = jnp.max(top[...], axis=1, keepdims=True)
        wide = jnp.broadcast_to(m, (ROWS, HD))
        top[...] = wide

        own_p = jnp.exp2((own - m) * EXP_SCALE).astype(bf16).astype(f32)
        own_v = jnp.concatenate([qs[d, :, w + HD : w + 2 * HD]] * GQ, axis=0).astype(f32)
        ones = jnp.ones((BLK, HD), bf16)

        def weigh(group, parts, codes):
            ps = []
            for u in range(parts):
                s = scores[group, :, u * BLK : (u + 1) * BLK]
                ps.append(jnp.exp2((s - top[...]) * EXP_SCALE).astype(bf16))
            p = jnp.concatenate(ps, axis=1)
            values = jnp.concatenate(
                [jnp.concatenate([block(code, slice(HD, KV2)), ones], axis=1) for code in codes], axis=0
            )
            return jnp.dot(p, values, preferred_element_type=f32)

        start = jnp.concatenate([own_p * own_v, jnp.broadcast_to(own_p, (ROWS, HD))], axis=1)
        acc[...] = start + weigh(STEPS, STEP, codes[:STEP]) + weigh(STEPS + 1, TAIL - STEP, codes[STEP:])

        def second_pass(g, carry):
            acc[...] += weigh(g, STEP, [table[g * STEP + u] for u in range(STEP)])
            return carry

        lax.fori_loop(0, full, second_pass, 0)
        out = (acc[:, :HD] / acc[:, HD:]).astype(bf16)
        for e in range(N_X):

            @pl.when(d == e)
            def _():
                for g in range(GQ):
                    outs[e][:, g * HD : (g + 1) * HD] = out[g * R_DEV : (g + 1) * R_DEV]

        return carry

    lax.fori_loop(0, N_X, visit, 0)


def read(scalars, kv_arrays, q_arrays):
    out = jax.ShapeDtypeStruct((R_DEV, GQ * HD), bf16)
    n_arr = len(kv_arrays)
    hbm = pl.BlockSpec(memory_space=pl.ANY)
    vmem = pl.BlockSpec(memory_space=pltpu.VMEM)
    return pl.pallas_call(
        reader_kernel,
        out_shape=(out,) * N_X,
        in_specs=[pl.BlockSpec(memory_space=pltpu.SMEM)] + [hbm] * (n_arr + N_X),
        out_specs=(vmem,) * N_X,
        scratch_shapes=[
            pltpu.VMEM((PIECES, PIECE, KV2), bf16),
            pltpu.VMEM((N_X, R_DEV, QW), bf16),
            pltpu.VMEM((STEPS + 2, ROWS, STEP * BLK), f32),
            pltpu.VMEM((ROWS, HD), f32),
            pltpu.VMEM((ROWS, KV2), f32),
            pltpu.SMEM((N_SEQ * KEEP + KEEP,), jnp.int32),
            pltpu.SMEM((N_SEQ,), jnp.int32),
            pltpu.SemaphoreType.DMA((N_X + n_arr,)),
        ],
        compiler_params=pltpu.CompilerParams(vmem_limit_bytes=56 << 20),
        name="reader",
    )(scalars, *kv_arrays, *q_arrays)


def ring(a, b, shift):
    left_a = shift(a, 1)
    right_b = shift(b, -1)
    left_b = shift(b, 1)
    right_a = shift(a, -1)
    far_a = shift(left_a, 1)
    far_b = shift(right_b, -1)
    return (left_a, left_b), (right_a, right_b), (far_a, far_b)


def on_device(
    passage_q,
    passage_k,
    passage_v,
    kept,
    context_map,
    recompute_pos,
    recompute_q,
    recompute_k,
    recompute_v,
):
    y = lax.axis_index("grp")
    s = lax.axis_index("seq")
    x, z, c = s // (N_Z * 2), (s // 2) % N_Z, s % 2
    scalars = jnp.concatenate([kept[0], x[None].astype(jnp.int32)])
    place = (recompute_pos[0] % PLEN).reshape(R_DEV, 1)
    a, b, *queries = pack(
        scalars, passage_k, passage_v, recompute_q[0], recompute_k[0], recompute_v[0], place
    )
    left, right, far = ring(a, b, shift_y)
    passage_out = encode(passage_q, passage_k, passage_v)
    q_arrays = [queries[0]] + [shift_seq(queries[d], dx=d) for d in range(1, N_X)]

    source = context_map[0, 0] // N_SEQ
    rel = (source - y) % N_GRP

    def pick(e):
        own = (a, b)[e]
        return jnp.where(rel == 0, own, jnp.where(rel == 1, right[e], jnp.where(rel == 2, far[e], left[e])))

    chosen = jnp.concatenate([pick(0), pick(1)], axis=0)
    pieces = [lax.dynamic_index_in_dim(chosen, (x + d) % N_X, 0, keepdims=True) for d in range(N_X)]
    moved = [pieces[0]] + [shift_seq(pieces[d], dx=d) for d in range(1, N_X)]
    wa = jnp.concatenate(moved[:2], axis=0)
    wb = jnp.concatenate(moved[2:], axis=0)
    zl, zr, zf = ring(wa, wb, lambda t, k: shift_seq(t, dz=k))
    mine = [wa, wb, zr[0], zr[1], zf[0], zf[1], zl[0], zl[1]]
    other = [shift_seq(t, dc=1) for t in mine]
    where = jnp.stack([x, z, c]).astype(jnp.int32)
    outs = read(where, mine + other, q_arrays)
    back = [outs[0]] + [shift_seq(outs[d], dx=-d) for d in range(1, N_X)]

    def head(h):
        d = (h - x) % N_X
        return jnp.where(d == 0, back[0], jnp.where(d == 1, back[1], jnp.where(d == 2, back[2], back[3])))

    reader_rows = jnp.concatenate([head(h) for h in range(KVH)], axis=1)
    return (passage_out, reader_rows[None])


def solution(mesh):
    return jax.shard_map(
        on_device,
        mesh=mesh,
        in_specs=(
            P(("grp", "seq"), None),
            P(("grp", "seq"), None),
            P(("grp", "seq"), None),
            P(("grp", "seq"), None),
            P("grp", "seq"),
            P("grp", "seq"),
            P("grp", "seq", None),
            P("grp", "seq", None),
            P("grp", "seq", None),
        ),
        out_specs=(P(("grp", "seq"), None), P("grp", "seq", None)),
        check_vma=False,
    )
```

```python
import functools
import math

import jax
import jax.numpy as jnp
from jax import lax
from jax.experimental import pallas as pl
from jax.experimental.pallas import tpu as pltpu
from jax.sharding import PartitionSpec as P


HQ = 32
KVH = 4
GQ = HQ // KVH
HD = 128
PLEN = 512
BLK = 128
KEEP = 3
NBLK = PLEN // BLK
R_DEV = 64
N_GRP = 4
N_X = 4
N_Z = 4
N_SEQ = 32
ROW = BLK // 2
META = KEEP * ROW
PIECE = META + 16
KV2 = 2 * HD
QW = GQ * HD + 4 * HD
ROWS = GQ * R_DEV
EXP_SCALE = HD ** (-0.5) * math.log2(math.e)
FAR = 100
STEP = 8
PIECES = N_SEQ


NT = (((1,), (1,)), ((), ()))
bf16 = jnp.bfloat16
f32 = jnp.float32


def seq_of(x, z, c):
    return x * (N_Z * 2) + z * 2 + c


def shift_y(a, k):
    return lax.ppermute(a, "grp", [(i, (i + k) % N_GRP) for i in range(N_GRP)])


def seq_pairs(dx, dz, dc):
    return [
        (seq_of(x, z, c), seq_of((x + dx) % N_X, (z + dz) % N_Z, (c + dc) % 2))
        for x in range(N_X)
        for z in range(N_Z)
        for c in range(2)
    ]


def shift_seq(a, dx=0, dz=0, dc=0):
    return lax.ppermute(a, "seq", seq_pairs(dx, dz, dc))


def place_of():
    s = lax.axis_index("seq")
    return s // (N_Z * 2), lax.rem(s // 2, N_Z), lax.rem(s, 2)


def pack_kernel(half, kept_ref, k_ref, v_ref, out):
    kept = [kept_ref[0, b] for b in range(NBLK)]
    before = [0]
    for b in range(NBLK):
        before.append(before[-1] + kept[b])
    count = before[NBLK]
    row = lax.broadcasted_iota(jnp.int32, (16, HD), 0)
    meta = jnp.where(row == 0, count, FAR)
    for j in range(KEEP):
        block = 0
        for b in range(NBLK):
            block = block + jnp.where((kept[b] > 0) & (before[b] == j), b, 0)
        meta = jnp.where(row == 1 + j, jnp.where(j < count, block, FAR), meta)
        start = pl.multiple_of(block * BLK + half * ROW, ROW)
        for h in range(KVH):
            cols = slice(h * HD, (h + 1) * HD)
            rows = slice(j * ROW, (j + 1) * ROW)
            out[h, rows, :HD] = k_ref[pl.ds(start, ROW), cols]
            out[h, rows, HD:] = v_ref[pl.ds(start, ROW), cols]
    meta = meta.astype(f32).astype(bf16)
    for h in range(KVH):
        out[h, META:, :HD] = meta
        out[h, META:, HD:] = meta


def pack(half, kept, k, v):
    vmem = pl.BlockSpec(memory_space=pltpu.VMEM)
    return pl.pallas_call(
        functools.partial(pack_kernel, half),
        out_shape=jax.ShapeDtypeStruct((KVH, PIECE, KV2), bf16),
        in_specs=[pl.BlockSpec(memory_space=pltpu.SMEM), vmem, vmem],
        out_specs=vmem,
    )(kept, k, v)


def query_kernel(pos_ref, q_ref, rk_ref, rv_ref, q0, q1, q2, q3):
    x, z, c = place_of()
    row = lax.broadcasted_iota(jnp.int32, (R_DEV, R_DEV), 0)
    col = lax.broadcasted_iota(jnp.int32, (R_DEV, R_DEV), 1)
    pos = (pos_ref[...] - seq_of(x, z, c) * PLEN).astype(f32)
    pos = jnp.sum(jnp.where(row == col, pos, 0.0), axis=1, keepdims=True).astype(jnp.int32)
    high = jnp.broadcast_to(pos // 16, (R_DEV, HD)).astype(f32).astype(bf16)
    low = jnp.broadcast_to(pos % 16, (R_DEV, HD)).astype(f32).astype(bf16)
    w = GQ * HD
    for d, out in enumerate((q0, q1, q2, q3)):
        h = lax.rem(x + d, N_X)
        out[:, :w] = q_ref[:, pl.ds(pl.multiple_of(h * w, w), w)]
        cols = pl.ds(pl.multiple_of(h * HD, HD), HD)
        out[:, w : w + HD] = rk_ref[:, cols]
        out[:, w + HD : w + 2 * HD] = rv_ref[:, cols]
        out[:, w + 2 * HD : w + 3 * HD] = high
        out[:, w + 3 * HD :] = low


def split_queries(pos, q, rk, rv):
    query = jax.ShapeDtypeStruct((R_DEV, QW), bf16)
    vmem = pl.BlockSpec(memory_space=pltpu.VMEM)
    return pl.pallas_call(
        query_kernel,
        out_shape=(query,) * N_X,
        in_specs=[vmem] * 4,
        out_specs=(vmem,) * N_X,
        name="queries",
    )(pos, q, rk, rv)


def passage_kernel(q_ref, k_ref, v_ref, o_ref):
    ones = jnp.ones((PLEN, HD), bf16)
    values = jnp.concatenate([v_ref[...], ones], axis=1)
    keys = k_ref[...]
    row = lax.broadcasted_iota(jnp.int32, (BLK, BLK), 0)
    col = lax.broadcasted_iota(jnp.int32, (BLK, BLK), 1)
    hidden = jnp.concatenate([col > row] * GQ, axis=0)
    for i in range(NBLK):
        rows = slice(i * BLK, (i + 1) * BLK)
        n = (i + 1) * BLK
        q = jnp.concatenate([q_ref[rows, g * HD : (g + 1) * HD] for g in range(GQ)], axis=0)
        s = lax.dot_general(q, keys[:n], NT, preferred_element_type=f32)
        last = jnp.where(hidden, -jnp.inf, s[:, n - BLK :])
        s = last if i == 0 else jnp.concatenate([s[:, : n - BLK], last], axis=1)
        m = jnp.max(s, axis=1, keepdims=True)
        p = jnp.exp2((s - m) * EXP_SCALE).astype(bf16)
        mixed = jnp.dot(p, values[:n], preferred_element_type=f32)
        out = (mixed[:, :HD] / mixed[:, HD:]).astype(bf16)
        for g in range(GQ):
            o_ref[rows, g * HD : (g + 1) * HD] = out[g * BLK : (g + 1) * BLK]


def encode(q, k, v, first, heads, done):
    w = GQ * HD
    blocks = [
        pl.BlockSpec((PLEN, w), lambda h: (0, first + h)),
        pl.BlockSpec((PLEN, HD), lambda h: (0, first + h)),
        pl.BlockSpec((PLEN, HD), lambda h: (0, first + h)),
    ]
    operands = [q, k, v]
    if done is not None:
        blocks.append(pl.BlockSpec(memory_space=pl.ANY))
        operands.append(done)

    def kernel(q_ref, k_ref, v_ref, *rest):
        passage_kernel(q_ref, k_ref, v_ref, rest[-1])

    return pl.pallas_call(
        kernel,
        out_shape=jax.ShapeDtypeStruct((PLEN, HQ * HD), bf16),
        grid=(heads,),
        in_specs=blocks,
        out_specs=pl.BlockSpec((PLEN, w), lambda h: (0, first + h)),
        input_output_aliases={} if done is None else {3: 0},
        cost_estimate=pl.CostEstimate(
            flops=heads * 4 * PLEN * PLEN * w,
            bytes_accessed=heads * (9 << 18),
            transcendentals=heads * GQ * PLEN * PLEN,
        ),
    )(*operands)


def reader_kernel(half, *refs):
    arrays = 2 * N_Z
    kv_in, refs = refs[:arrays], refs[arrays:]
    q_in, refs = refs[:N_X], refs[N_X:]
    if half:
        acc_in, state_in = refs[:2]
        outs, refs = refs[2 : 2 + N_X], refs[2 + N_X :]
    else:
        acc_out, state_out = refs[:2]
        refs = refs[2:]
    kv, qs, scores, top, acc, codes, bases, starts, sems = refs
    x, z, c = place_of()
    copies = [
        pltpu.make_async_copy(kv_in[a], kv.at[pl.ds(N_X * a, N_X)], sems.at[N_X + a]) for a in range(arrays)
    ]
    copies += [pltpu.make_async_copy(q_in[d], qs.at[d], sems.at[d]) for d in range(N_X)]
    for copy in copies:
        copy.start()
    for copy in copies:
        copy.wait()

    n = jnp.int32(0)
    for t in range(N_SEQ):
        tx, tz, tc = t // (N_Z * 2), (t // 2) % N_Z, t % 2
        piece = lax.rem(c + tc, 2) * 16 + lax.rem(tz - z + N_Z, N_Z) * 4 + lax.rem(x - tx + N_X, N_X)
        count = jnp.max(kv[piece, META : META + 1, :HD].astype(f32)).astype(jnp.int32)
        starts[t] = n
        for j in range(KEEP):
            codes[n + j] = piece * KEEP + j
            bases[n + j] = t * PLEN
        n = n + count
    starts[N_SEQ] = n
    for j in range(2 * STEP):
        codes[n + j] = 0
        bases[n + j] = FAR * PLEN

    lane = lax.broadcasted_iota(jnp.int32, (1, 2 * ROW), 1)
    w = GQ * HD

    def block(code, cols):
        piece = code // KEEP
        first = pl.multiple_of(lax.rem(code, KEEP) * ROW, ROW)
        return kv[piece, pl.ds(first, ROW), cols]

    def gather(g, count, cols):
        return jnp.concatenate([block(codes[g * STEP + u], cols) for u in range(count * STEP)], axis=0)

    def visit(d, carry):
        shard = seq_of(lax.rem(x - d + N_X, N_X), z, c)
        q = jnp.concatenate([qs[d, :, g * HD : (g + 1) * HD] for g in range(GQ)], axis=0)
        begin = starts[shard]
        end = starts[shard + 1]
        for j in range(KEEP):

            @pl.when(begin + j < end)
            def _():
                number = jnp.max(kv[d, META + 1 + j : META + 2 + j, :HD].astype(f32)).astype(jnp.int32)
                bases[begin + j] = shard * PLEN + number * BLK + half * ROW

        if half:
            old = jnp.broadcast_to(state_in[d, :, 0:1], (ROWS, HD))
        else:
            own_k = jnp.concatenate([qs[d, :, w : w + HD]] * GQ, axis=0).astype(f32)
            own = jnp.sum(q.astype(f32) * own_k, axis=1, keepdims=True) * EXP_SCALE
            old = jnp.broadcast_to(own, (ROWS, HD))
        top[...] = old

        def first_pass(g, count, masked):
            s = lax.dot_general(q, gather(g, count, slice(0, HD)), NT, preferred_element_type=f32)
            best = top[...]
            for u in range(count * STEP // 2):
                part = s[:, u * HD : (u + 1) * HD] * EXP_SCALE
                if masked:
                    b0 = bases[g * STEP + 2 * u]
                    b1 = bases[g * STEP + 2 * u + 1] - ROW
                    spot = (jnp.where(lane < ROW, b0, b1) + lane).astype(f32)
                    high = qs[d, :, w + 2 * HD : w + 3 * HD].astype(f32)
                    place = high * 16 + qs[d, :, w + 3 * HD :].astype(f32)
                    spot = spot - (shard * PLEN).astype(f32)
                    part = jnp.concatenate(
                        [
                            jnp.where(spot < place, part[r * R_DEV : (r + 1) * R_DEV], -jnp.inf)
                            for r in range(GQ)
                        ],
                        axis=0,
                    )
                half_step = STEP // 2
                at = slice((u % half_step) * HD, (u % half_step + 1) * HD)
                scores[g + u // half_step, :, at] = part
                best = jnp.maximum(best, part)
            top[...] = best

        pairs = begin // (2 * STEP)
        groups = (end + STEP - 1) // STEP

        @pl.loop(0, pairs)
        def _(i):
            first_pass(2 * i, 2, False)

        @pl.loop(2 * pairs, groups)
        def _(g):
            first_pass(g, 1, True)

        m = jnp.max(top[...], axis=1, keepdims=True)
        wide = jnp.broadcast_to(m, (ROWS, HD))
        top[...] = wide
        if half:
            alpha = jnp.exp2(old - wide)
            acc[:, :HD] = acc_in[d] * alpha
            acc[:, HD:] = jnp.where(lane == 0, alpha * jnp.broadcast_to(state_in[d, :, ROW : ROW + 1], (ROWS, HD)), 0.0)
        else:
            alpha = jnp.exp2(old - wide).astype(bf16).astype(f32)
            own_v = jnp.concatenate([qs[d, :, w + HD : w + 2 * HD]] * GQ, axis=0).astype(f32)
            acc[:, :HD] = alpha * own_v
            acc[:, HD:] = jnp.where(lane == 0, alpha, 0.0)

        def second_pass(g, count):
            ps = []
            total = acc[:, HD:]
            for u in range(count * STEP // 2):
                half_step = STEP // 2
                at = slice((u % half_step) * HD, (u % half_step + 1) * HD)
                p = jnp.exp2(scores[g + u // half_step, :, at] - top[...]).astype(bf16)
                total = total + p.astype(f32)
                ps.append(p)
            acc[:, HD:] = total
            p = jnp.concatenate(ps, axis=1)
            acc[:, :HD] += jnp.dot(p, gather(g, count, slice(HD, KV2)), preferred_element_type=f32)

        @pl.loop(0, groups // 2)
        def _(i):
            second_pass(2 * i, 2)

        @pl.when(groups % 2 == 1)
        def _():
            second_pass(groups - 1, 1)

        total = jnp.sum(acc[:, HD:], axis=1, keepdims=True)
        if half:
            out = (acc[:, :HD] / total).astype(bf16)
            for e in range(N_X):

                @pl.when(d == e)
                def _():
                    for g in range(GQ):
                        outs[e][:, g * HD : (g + 1) * HD] = out[g * R_DEV : (g + 1) * R_DEV]

        else:
            acc_out[d] = acc[:, :HD]
            state_out[d] = jnp.where(lane < ROW, top[...], total)
        return carry

    lax.fori_loop(0, N_X, visit, 0)


def read(half, kv_arrays, q_arrays, state):
    out = jax.ShapeDtypeStruct((R_DEV, GQ * HD), bf16)
    kept_state = jax.ShapeDtypeStruct((N_X, ROWS, HD), f32)
    arrays = len(kv_arrays)
    hbm = pl.BlockSpec(memory_space=pl.ANY)
    vmem = pl.BlockSpec(memory_space=pltpu.VMEM)
    most = N_SEQ * KEEP
    return pl.pallas_call(
        functools.partial(reader_kernel, half),
        out_shape=(out,) * N_X if half else (kept_state,) * 2,
        in_specs=[hbm] * (arrays + N_X) + [vmem] * len(state),
        out_specs=(vmem,) * (N_X if half else 2),
        scratch_shapes=[
            pltpu.VMEM((PIECES, PIECE, KV2), bf16),
            pltpu.VMEM((N_X, R_DEV, QW), bf16),
            pltpu.VMEM((most // STEP, ROWS, STEP * ROW), f32),
            pltpu.VMEM((ROWS, HD), f32),
            pltpu.VMEM((ROWS, KV2), f32),
            pltpu.SMEM((most + 2 * STEP,), jnp.int32),
            pltpu.SMEM((most + 2 * STEP,), jnp.int32),
            pltpu.SMEM((N_SEQ + 1,), jnp.int32),
            pltpu.SemaphoreType.DMA((N_X + arrays,)),
        ],
        compiler_params=pltpu.CompilerParams(vmem_limit_bytes=40 << 20),
        cost_estimate=pl.CostEstimate(flops=5 << 30, bytes_accessed=8 << 20, transcendentals=6 << 20),
    )(*kv_arrays, *q_arrays, *state)


def around(a, shift):
    return [shift(a, k) for k in (3, 1, 2)]


def whole(
    passage_q,
    passage_k,
    passage_v,
    kept,
    context_map,
    recompute_pos,
    recompute_q,
    recompute_k,
    recompute_v,
):
    y = lax.axis_index("grp")
    x, _, _ = place_of()
    source = context_map[0, 0] // N_SEQ
    rel = (source - y) % N_GRP

    def across_x(own):
        pieces = [lax.dynamic_index_in_dim(own, (x + d) % N_X, 0, keepdims=True) for d in range(N_X)]
        moved = [pieces[0]] + [shift_seq(pieces[d], dx=d) for d in range(1, N_X)]
        return jnp.concatenate(moved, axis=0)

    def choose(offset, own, others):
        up, down, far = others
        return jnp.where(offset == 0, own, jnp.where(offset == 1, up, jnp.where(offset == 2, far, down)))

    def around_z(near):
        up, down, far = around(near, lambda t, k: shift_seq(t, dz=k))
        return [near, up, far, down]

    def swap(t):
        return shift_seq(t, dc=1)

    fence = lax.optimization_barrier
    first = pack(0, kept, passage_k, passage_v)
    near0 = around(first, shift_y)
    second = pack(1, kept, passage_k, passage_v)
    near1 = around(second, shift_y)
    queries = split_queries(recompute_pos, recompute_q[0], recompute_k[0], recompute_v[0])
    q_arrays = [queries[0]] + [shift_seq(queries[d], dx=d) for d in range(1, N_X)]
    passage_out = encode(passage_q, passage_k, passage_v, 0, 2, None)
    rel, passage_out, q_arrays = fence((rel, passage_out, q_arrays))

    mine0 = around_z(across_x(choose(rel, first, near0)))
    other0 = [swap(mine0[0])]
    rel, passage_out, other0 = fence((rel, passage_out, other0))
    passage_out = encode(passage_q, passage_k, passage_v, 2, 2, passage_out)
    rel, passage_out = fence((rel, passage_out))
    mine1 = around_z(across_x(choose(rel, second, near1)))
    kv0 = mine0 + other0 + [swap(t) for t in mine0[1:]]
    state = read(0, kv0, q_arrays, ())
    other1 = [swap(mine1[0])]
    state, other1, far1 = fence((state, other1, mine1[1:]))
    mine1 = mine1[:1] + far1
    kv1 = mine1 + other1 + [swap(t) for t in far1]
    outs = read(1, kv1, q_arrays, state)
    back = [outs[0]] + [shift_seq(outs[d], dx=-d) for d in range(1, N_X)]

    def head(h):
        d = (h - x) % N_X
        return jnp.where(d == 0, back[0], jnp.where(d == 1, back[1], jnp.where(d == 2, back[2], back[3])))

    reader_rows = jnp.concatenate([head(h) for h in range(KVH)], axis=1)
    return (passage_out, reader_rows[None])


def solution(mesh):
    return jax.shard_map(
        whole,
        mesh=mesh,
        in_specs=(
            P(("grp", "seq"), None),
            P(("grp", "seq"), None),
            P(("grp", "seq"), None),
            P(("grp", "seq"), None),
            P("grp", "seq"),
            P("grp", "seq"),
            P("grp", "seq", None),
            P("grp", "seq", None),
            P("grp", "seq", None),
        ),
        out_specs=(P(("grp", "seq"), None), P("grp", "seq", None)),
        check_vma=False,
    )
```

```python
import functools
import math

import jax
import jax.numpy as jnp
from jax import lax
from jax.experimental import pallas as pl
from jax.experimental.pallas import tpu as pltpu
from jax.sharding import PartitionSpec as P


HQ = 32
KVH = 4
GQ = HQ // KVH
HD = 128
PLEN = 512
BLK = 128
KEEP = 3
NBLK = PLEN // BLK
R_DEV = 64
N_GRP = 4
N_X = 4
N_Z = 4
N_SEQ = 32
ROW = BLK // 2
META = KEEP * ROW
PIECE = META + 16
KV2 = 2 * HD
QW = GQ * HD + 4 * HD
ROWS = GQ * R_DEV
EXP_SCALE = HD ** (-0.5) * math.log2(math.e)
FAR = 100
STEP = 8
PIECES = N_SEQ


NT = (((1,), (1,)), ((), ()))
bf16 = jnp.bfloat16
f32 = jnp.float32


def seq_of(x, z, c):
    return x * (N_Z * 2) + z * 2 + c


def shift_y(a, k):
    return lax.ppermute(a, "grp", [(i, (i + k) % N_GRP) for i in range(N_GRP)])


def seq_pairs(dx, dz, dc):
    return [
        (seq_of(x, z, c), seq_of((x + dx) % N_X, (z + dz) % N_Z, (c + dc) % 2))
        for x in range(N_X)
        for z in range(N_Z)
        for c in range(2)
    ]


def shift_seq(a, dx=0, dz=0, dc=0):
    return lax.ppermute(a, "seq", seq_pairs(dx, dz, dc))


def place_of():
    s = lax.axis_index("seq")
    return s // (N_Z * 2), lax.rem(s // 2, N_Z), lax.rem(s, 2)


def pack_kernel(half, kept_ref, k_ref, v_ref, out):
    kept = [kept_ref[0, b] for b in range(NBLK)]
    before = [0]
    for b in range(NBLK):
        before.append(before[-1] + kept[b])
    count = before[NBLK]
    row = lax.broadcasted_iota(jnp.int32, (16, HD), 0)
    meta = jnp.where(row == 0, count, FAR)
    for j in range(KEEP):
        block = 0
        for b in range(NBLK):
            block = block + jnp.where((kept[b] > 0) & (before[b] == j), b, 0)
        meta = jnp.where(row == 1 + j, jnp.where(j < count, block, FAR), meta)
        start = pl.multiple_of(block * BLK + half * ROW, ROW)
        for h in range(KVH):
            cols = slice(h * HD, (h + 1) * HD)
            rows = slice(j * ROW, (j + 1) * ROW)
            out[h, rows, :HD] = k_ref[pl.ds(start, ROW), cols]
            out[h, rows, HD:] = v_ref[pl.ds(start, ROW), cols]
    meta = meta.astype(f32).astype(bf16)
    for h in range(KVH):
        out[h, META:, :HD] = meta
        out[h, META:, HD:] = meta


def pack(half, kept, k, v):
    vmem = pl.BlockSpec(memory_space=pltpu.VMEM)
    return pl.pallas_call(
        functools.partial(pack_kernel, half),
        out_shape=jax.ShapeDtypeStruct((KVH, PIECE, KV2), bf16),
        in_specs=[pl.BlockSpec(memory_space=pltpu.SMEM), vmem, vmem],
        out_specs=vmem,
    )(kept, k, v)


def query_kernel(pos_ref, q_ref, rk_ref, rv_ref, q0, q1, q2, q3):
    x, z, c = place_of()
    row = lax.broadcasted_iota(jnp.int32, (R_DEV, R_DEV), 0)
    col = lax.broadcasted_iota(jnp.int32, (R_DEV, R_DEV), 1)
    pos = (pos_ref[...] - seq_of(x, z, c) * PLEN).astype(f32)
    pos = jnp.sum(jnp.where(row == col, pos, 0.0), axis=1, keepdims=True).astype(jnp.int32)
    high = jnp.broadcast_to(pos // 16, (R_DEV, HD)).astype(f32).astype(bf16)
    low = jnp.broadcast_to(pos % 16, (R_DEV, HD)).astype(f32).astype(bf16)
    w = GQ * HD
    for d, out in enumerate((q0, q1, q2, q3)):
        h = lax.rem(x + d, N_X)
        out[:, :w] = q_ref[:, pl.ds(pl.multiple_of(h * w, w), w)]
        cols = pl.ds(pl.multiple_of(h * HD, HD), HD)
        out[:, w : w + HD] = rk_ref[:, cols]
        out[:, w + HD : w + 2 * HD] = rv_ref[:, cols]
        out[:, w + 2 * HD : w + 3 * HD] = high
        out[:, w + 3 * HD :] = low


def split_queries(pos, q, rk, rv):
    query = jax.ShapeDtypeStruct((R_DEV, QW), bf16)
    vmem = pl.BlockSpec(memory_space=pltpu.VMEM)
    return pl.pallas_call(
        query_kernel,
        out_shape=(query,) * N_X,
        in_specs=[vmem] * 4,
        out_specs=(vmem,) * N_X,
        name="queries",
    )(pos, q, rk, rv)


def passage_kernel(q_ref, k_ref, v_ref, o_ref):
    ones = jnp.ones((PLEN, HD), bf16)
    values = jnp.concatenate([v_ref[...], ones], axis=1)
    keys = k_ref[...]
    row = lax.broadcasted_iota(jnp.int32, (BLK, BLK), 0)
    col = lax.broadcasted_iota(jnp.int32, (BLK, BLK), 1)
    hidden = jnp.concatenate([col > row] * GQ, axis=0)
    for i in range(NBLK):
        rows = slice(i * BLK, (i + 1) * BLK)
        n = (i + 1) * BLK
        q = jnp.concatenate([q_ref[rows, g * HD : (g + 1) * HD] for g in range(GQ)], axis=0)
        s = lax.dot_general(q, keys[:n], NT, preferred_element_type=f32)
        last = jnp.where(hidden, -jnp.inf, s[:, n - BLK :])
        s = last if i == 0 else jnp.concatenate([s[:, : n - BLK], last], axis=1)
        m = jnp.max(s, axis=1, keepdims=True)
        p = jnp.exp2((s - m) * EXP_SCALE).astype(bf16)
        mixed = jnp.dot(p, values[:n], preferred_element_type=f32)
        out = (mixed[:, :HD] / mixed[:, HD:]).astype(bf16)
        for g in range(GQ):
            o_ref[rows, g * HD : (g + 1) * HD] = out[g * BLK : (g + 1) * BLK]


def encode(q, k, v, first, heads, done):
    w = GQ * HD
    blocks = [
        pl.BlockSpec((PLEN, w), lambda h: (0, first + h)),
        pl.BlockSpec((PLEN, HD), lambda h: (0, first + h)),
        pl.BlockSpec((PLEN, HD), lambda h: (0, first + h)),
    ]
    operands = [q, k, v]
    if done is not None:
        blocks.append(pl.BlockSpec(memory_space=pl.ANY))
        operands.append(done)

    def kernel(q_ref, k_ref, v_ref, *rest):
        passage_kernel(q_ref, k_ref, v_ref, rest[-1])

    return pl.pallas_call(
        kernel,
        out_shape=jax.ShapeDtypeStruct((PLEN, HQ * HD), bf16),
        grid=(heads,),
        in_specs=blocks,
        out_specs=pl.BlockSpec((PLEN, w), lambda h: (0, first + h)),
        input_output_aliases={} if done is None else {3: 0},
        cost_estimate=pl.CostEstimate(
            flops=heads * 4 * PLEN * PLEN * w,
            bytes_accessed=heads * (9 << 18),
            transcendentals=heads * GQ * PLEN * PLEN,
        ),
    )(*operands)


def reader_kernel(half, *refs):
    arrays = 2 * N_Z
    kv_in, refs = refs[:arrays], refs[arrays:]
    q_in, refs = refs[:N_X], refs[N_X:]
    if half:
        mixes, stats = refs[:2]
        outs, refs = refs[2 : 2 + N_X], refs[2 + N_X :]
    else:
        mixes, stats = refs[:2]
        refs = refs[2:]
    kv, keys, values, qs, query, place, olds, scores, top, acc, bases, starts, sems = refs
    x, z, c = place_of()
    copies = [
        pltpu.make_async_copy(kv_in[a], kv.at[pl.ds(N_X * a, N_X)], sems.at[N_X + a]) for a in range(arrays)
    ]
    copies += [
        pltpu.make_async_copy(q_in[d], qs.at[lax.rem(x - d + N_X, N_X)], sems.at[d]) for d in range(N_X)
    ]
    for copy in copies:
        copy.start()
    for copy in copies:
        copy.wait()

    n = jnp.int32(0)
    for t in range(N_SEQ):
        tx, tz, tc = t // (N_Z * 2), (t // 2) % N_Z, t % 2
        piece = lax.rem(c + tc, 2) * 16 + lax.rem(tz - z + N_Z, N_Z) * 4 + lax.rem(x - tx + N_X, N_X)
        count = jnp.max(kv[piece, META : META + 1, :HD].astype(f32)).astype(jnp.int32)
        starts[t] = n
        at = pl.ds(pl.multiple_of(n * ROW, ROW), META)
        keys[at, :] = kv[piece, :META, :HD]
        values[at, :] = kv[piece, :META, HD:]
        for j in range(KEEP):
            bases[n + j] = t * PLEN
        n = n + count
    starts[N_SEQ] = n
    values[pl.ds(pl.multiple_of(n * ROW, ROW), 2 * STEP * ROW), :] = jnp.zeros((2 * STEP * ROW, HD), bf16)
    for j in range(2 * STEP):
        bases[n + j] = FAR * PLEN

    lane = lax.broadcasted_iota(jnp.int32, (1, 2 * ROW), 1)
    w = GQ * HD

    def gather(ref, g):
        return ref[pl.ds(pl.multiple_of(g * STEP * ROW, STEP * ROW), STEP * ROW), :]

    def columns(pair, first, width):
        parts = [qs[2 * pair + r, :, first : first + width] for r in range(2)]
        return jnp.concatenate([parts[r] for r in range(2) for _ in range(GQ)], axis=0)

    def visit(pair, carry):
        shards = [seq_of(2 * pair + r, z, c) for r in range(2)]
        begins = [starts[shards[r]] for r in range(2)]
        ends = [starts[shards[r] + 1] for r in range(2)]
        for r in range(2):
            piece = lax.rem(x - (2 * pair + r) + N_X, N_X)
            for j in range(KEEP):

                @pl.when(begins[r] + j < ends[r])
                def _():
                    number = jnp.max(kv[piece, META + 1 + j : META + 2 + j, :HD].astype(f32)).astype(jnp.int32)
                    bases[begins[r] + j] = shards[r] * PLEN + number * BLK + half * ROW

            for g in range(GQ):
                rows = slice((r * GQ + g) * R_DEV, (r * GQ + g + 1) * R_DEV)
                query[rows, :] = qs[2 * pair + r, :, g * HD : (g + 1) * HD]
        high = columns(pair, w + 2 * HD, HD).astype(f32)
        low = columns(pair, w + 3 * HD, HD).astype(f32)
        row = lax.broadcasted_iota(jnp.int32, (2 * ROWS, 1), 0)
        first = jnp.where(row < ROWS, shards[0] * PLEN, shards[1] * PLEN).astype(f32)
        place[...] = high * 16 + low + first

        if half:
            state = jnp.concatenate([stats[2 * pair + r] for r in range(2)], axis=0)
            old = jnp.broadcast_to(state[:, 0:1], (2 * ROWS, HD))
            olds[...] = old
        else:
            own_k = columns(pair, w, HD).astype(f32)
            own = jnp.sum(query[...].astype(f32) * own_k, axis=1, keepdims=True) * EXP_SCALE
            old = jnp.broadcast_to(own, (2 * ROWS, HD))
            olds[...] = old
        top[...] = old

        def first_pass(g, rows, masked):
            s = lax.dot_general(query[rows, :], gather(keys, g), NT, preferred_element_type=f32)
            best = top[rows, :]
            for u in range(STEP // 2):
                part = s[:, u * HD : (u + 1) * HD] * EXP_SCALE
                if masked:
                    b0 = bases[g * STEP + 2 * u]
                    b1 = bases[g * STEP + 2 * u + 1] - ROW
                    spot = (jnp.where(lane < ROW, b0, b1) + lane).astype(f32)
                    part = jnp.where(spot < place[rows, :], part, -jnp.inf)
                scores[g, rows, u * HD : (u + 1) * HD] = part
                best = jnp.maximum(best, part)
            top[rows, :] = best

        everything, upper = slice(0, 2 * ROWS), slice(ROWS, 2 * ROWS)
        plain = begins[0] // STEP
        both = (ends[0] + STEP - 1) // STEP
        most = (ends[1] + STEP - 1) // STEP

        @pl.loop(0, plain)
        def _(g):
            first_pass(g, everything, False)

        @pl.loop(plain, both)
        def _(g):
            first_pass(g, everything, True)

        @pl.loop(both, most)
        def _(g):
            first_pass(g, upper, True)

        m = jnp.max(top[...], axis=1, keepdims=True)
        wide = jnp.broadcast_to(m, (2 * ROWS, HD))
        top[...] = wide
        if half:
            alpha = jnp.exp2(olds[...] - wide)
            mixed = jnp.concatenate([mixes[2 * pair + r] for r in range(2)], axis=0)
            state = jnp.concatenate([stats[2 * pair + r] for r in range(2)], axis=0)
            acc[:, :HD] = mixed * alpha
            acc[:, HD:] = jnp.where(
                lane == 0, alpha * jnp.broadcast_to(state[:, ROW : ROW + 1], (2 * ROWS, HD)), 0.0
            )
        else:
            alpha = jnp.exp2(olds[...] - wide).astype(bf16).astype(f32)
            acc[:, :HD] = alpha * columns(pair, w + HD, HD).astype(f32)
            acc[:, HD:] = jnp.where(lane == 0, alpha, 0.0)

        def second_pass(g, rows):
            ps = []
            total = acc[rows, HD:]
            for u in range(STEP // 2):
                p = jnp.exp2(scores[g, rows, u * HD : (u + 1) * HD] - top[rows, :])
                total = total + p
                ps.append(p.astype(bf16))
            acc[rows, HD:] = total
            p = jnp.concatenate(ps, axis=1)
            acc[rows, :HD] += jnp.dot(p, gather(values, g), preferred_element_type=f32)

        @pl.loop(0, both)
        def _(g):
            second_pass(g, everything)

        @pl.loop(both, most)
        def _(g):
            second_pass(g, upper)

        total = jnp.sum(acc[:, HD:], axis=1, keepdims=True)
        if half:
            out = (acc[:, :HD] / total).astype(bf16)
            for r in range(2):
                d = lax.rem(x - (2 * pair + r) + N_X, N_X)
                for e in range(N_X):

                    @pl.when(d == e)
                    def _():
                        for g in range(GQ):
                            rows = slice((r * GQ + g) * R_DEV, (r * GQ + g + 1) * R_DEV)
                            outs[e][:, g * HD : (g + 1) * HD] = out[rows]

        else:
            for r in range(2):
                rows = slice(r * ROWS, (r + 1) * ROWS)
                mixes[2 * pair + r] = acc[rows, :HD]
                stats[2 * pair + r] = jnp.where(lane < ROW, top[rows, :], total[rows])
        return carry

    lax.fori_loop(0, N_X // 2, visit, 0)


def read(half, kv_arrays, q_arrays, state):
    out = jax.ShapeDtypeStruct((R_DEV, GQ * HD), bf16)
    kept_state = jax.ShapeDtypeStruct((N_X, ROWS, HD), f32)
    arrays = len(kv_arrays)
    hbm = pl.BlockSpec(memory_space=pl.ANY)
    vmem = pl.BlockSpec(memory_space=pltpu.VMEM)
    most = N_SEQ * KEEP
    return pl.pallas_call(
        functools.partial(reader_kernel, half),
        out_shape=(out,) * N_X if half else (kept_state,) * 2,
        in_specs=[hbm] * (arrays + N_X) + [vmem] * len(state),
        out_specs=(vmem,) * (N_X if half else 2),
        scratch_shapes=[
            pltpu.VMEM((PIECES, PIECE, KV2), bf16),
            pltpu.VMEM(((most + 2 * STEP) * ROW, HD), bf16),
            pltpu.VMEM(((most + 2 * STEP) * ROW, HD), bf16),
            pltpu.VMEM((N_X, R_DEV, QW), bf16),
            pltpu.VMEM((2 * ROWS, HD), bf16),
            pltpu.VMEM((2 * ROWS, HD), f32),
            pltpu.VMEM((2 * ROWS, HD), f32),
            pltpu.VMEM((most // STEP, 2 * ROWS, STEP * ROW), f32),
            pltpu.VMEM((2 * ROWS, HD), f32),
            pltpu.VMEM((2 * ROWS, KV2), f32),
            pltpu.SMEM((most + 2 * STEP,), jnp.int32),
            pltpu.SMEM((N_SEQ + 1,), jnp.int32),
            pltpu.SemaphoreType.DMA((N_X + arrays,)),
        ],
        compiler_params=pltpu.CompilerParams(vmem_limit_bytes=44 << 20),
        cost_estimate=pl.CostEstimate(flops=5 << 30, bytes_accessed=8 << 20, transcendentals=6 << 20),
    )(*kv_arrays, *q_arrays, *state)


def around(a, shift):
    return [shift(a, k) for k in (3, 1, 2)]


def whole(
    passage_q,
    passage_k,
    passage_v,
    kept,
    context_map,
    recompute_pos,
    recompute_q,
    recompute_k,
    recompute_v,
):
    y = lax.axis_index("grp")
    x, _, _ = place_of()
    source = context_map[0, 0] // N_SEQ
    rel = (source - y) % N_GRP

    def across_x(own):
        pieces = [lax.dynamic_index_in_dim(own, (x + d) % N_X, 0, keepdims=True) for d in range(N_X)]
        moved = [pieces[0]] + [shift_seq(pieces[d], dx=d) for d in range(1, N_X)]
        return jnp.concatenate(moved, axis=0)

    def choose(offset, own, others):
        up, down, far = others
        return jnp.where(offset == 0, own, jnp.where(offset == 1, up, jnp.where(offset == 2, far, down)))

    def around_z(near):
        up, down, far = around(near, lambda t, k: shift_seq(t, dz=k))
        return [near, up, far, down]

    def swap(t):
        return shift_seq(t, dc=1)

    fence = lax.optimization_barrier
    first = pack(0, kept, passage_k, passage_v)
    near0 = around(first, shift_y)
    second = pack(1, kept, passage_k, passage_v)
    near1 = around(second, shift_y)
    queries = split_queries(recompute_pos, recompute_q[0], recompute_k[0], recompute_v[0])
    q_arrays = [queries[0]] + [shift_seq(queries[d], dx=d) for d in range(1, N_X)]
    passage_out = encode(passage_q, passage_k, passage_v, 0, 2, None)
    rel, passage_out, q_arrays = fence((rel, passage_out, q_arrays))

    here0 = across_x(choose(rel, first, near0))
    passage_out = encode(passage_q, passage_k, passage_v, 2, 1, passage_out)
    here0, passage_out = fence((here0, passage_out))
    mine0 = around_z(here0)
    other0 = [swap(mine0[0])]
    rel, other0 = fence((rel, other0))
    here1 = across_x(choose(rel, second, near1))
    passage_out = encode(passage_q, passage_k, passage_v, 3, 1, passage_out)
    here1, passage_out = fence((here1, passage_out))
    mine1 = around_z(here1)
    kv0 = mine0 + other0 + [swap(t) for t in mine0[1:]]
    state = read(0, kv0, q_arrays, ())
    other1 = [swap(mine1[0])]
    state, other1, far1 = fence((state, other1, mine1[1:]))
    mine1 = mine1[:1] + far1
    kv1 = mine1 + other1 + [swap(t) for t in far1]
    outs = read(1, kv1, q_arrays, state)
    back = [outs[0]] + [shift_seq(outs[d], dx=-d) for d in range(1, N_X)]

    def head(h):
        d = (h - x) % N_X
        return jnp.where(d == 0, back[0], jnp.where(d == 1, back[1], jnp.where(d == 2, back[2], back[3])))

    reader_rows = jnp.concatenate([head(h) for h in range(KVH)], axis=1)
    return (passage_out, reader_rows[None])


def solution(mesh):
    return jax.shard_map(
        whole,
        mesh=mesh,
        in_specs=(
            P(("grp", "seq"), None),
            P(("grp", "seq"), None),
            P(("grp", "seq"), None),
            P(("grp", "seq"), None),
            P("grp", "seq"),
            P("grp", "seq"),
            P("grp", "seq", None),
            P("grp", "seq", None),
            P("grp", "seq", None),
        ),
        out_specs=(P(("grp", "seq"), None), P("grp", "seq", None)),
        check_vma=False,
    )
```

```python
import functools
import math

import jax
import jax.numpy as jnp
from jax import lax
from jax.experimental import pallas as pl
from jax.experimental.pallas import tpu as pltpu
from jax.sharding import PartitionSpec as P


HQ = 32
KVH = 4
GQ = HQ // KVH
HD = 128
PLEN = 512
BLK = 128
KEEP = 3
NBLK = PLEN // BLK
R_DEV = 64
N_GRP = 4
N_X = 4
N_Z = 4
N_SEQ = 32
ROW = BLK // 2
META = KEEP * ROW
PIECE = META + 16
KV2 = 2 * HD
QW = GQ * HD + 4 * HD
ROWS = GQ * R_DEV
EXP_SCALE = HD ** (-0.5) * math.log2(math.e)
FAR = 100
STEP = 16
PIECES = N_SEQ


NT = (((1,), (1,)), ((), ()))
bf16 = jnp.bfloat16
f32 = jnp.float32


def seq_of(x, z, c):
    return x * (N_Z * 2) + z * 2 + c


def shift_y(a, k):
    return lax.ppermute(a, "grp", [(i, (i + k) % N_GRP) for i in range(N_GRP)])


def seq_pairs(dx, dz, dc):
    return [
        (seq_of(x, z, c), seq_of((x + dx) % N_X, (z + dz) % N_Z, (c + dc) % 2))
        for x in range(N_X)
        for z in range(N_Z)
        for c in range(2)
    ]


def shift_seq(a, dx=0, dz=0, dc=0):
    return lax.ppermute(a, "seq", seq_pairs(dx, dz, dc))


def place_of():
    s = lax.axis_index("seq")
    return s // (N_Z * 2), lax.rem(s // 2, N_Z), lax.rem(s, 2)


def pack_kernel(half, kept_ref, k_ref, v_ref, out):
    kept = [kept_ref[0, b] for b in range(NBLK)]
    before = [0]
    for b in range(NBLK):
        before.append(before[-1] + kept[b])
    count = before[NBLK]
    row = lax.broadcasted_iota(jnp.int32, (16, HD), 0)
    meta = jnp.where(row == 0, count, FAR)
    for j in range(KEEP):
        block = 0
        for b in range(NBLK):
            block = block + jnp.where((kept[b] > 0) & (before[b] == j), b, 0)
        meta = jnp.where(row == 1 + j, jnp.where(j < count, block, FAR), meta)
        start = pl.multiple_of(block * BLK + half * ROW, ROW)
        for h in range(KVH):
            cols = slice(h * HD, (h + 1) * HD)
            rows = slice(j * ROW, (j + 1) * ROW)
            out[h, rows, :HD] = k_ref[pl.ds(start, ROW), cols]
            out[h, rows, HD:] = v_ref[pl.ds(start, ROW), cols]
    meta = meta.astype(f32).astype(bf16)
    for h in range(KVH):
        out[h, META:, :HD] = meta
        out[h, META:, HD:] = meta


def pack(half, kept, k, v):
    vmem = pl.BlockSpec(memory_space=pltpu.VMEM)
    return pl.pallas_call(
        functools.partial(pack_kernel, half),
        out_shape=jax.ShapeDtypeStruct((KVH, PIECE, KV2), bf16),
        in_specs=[pl.BlockSpec(memory_space=pltpu.SMEM), vmem, vmem],
        out_specs=vmem,
    )(kept, k, v)


def query_kernel(pos_ref, q_ref, rk_ref, rv_ref, q0, q1, q2, q3):
    x, z, c = place_of()
    row = lax.broadcasted_iota(jnp.int32, (R_DEV, R_DEV), 0)
    col = lax.broadcasted_iota(jnp.int32, (R_DEV, R_DEV), 1)
    pos = (pos_ref[...] - seq_of(x, z, c) * PLEN).astype(f32)
    pos = jnp.sum(jnp.where(row == col, pos, 0.0), axis=1, keepdims=True).astype(jnp.int32)
    high = jnp.broadcast_to(pos // 16, (R_DEV, HD)).astype(f32).astype(bf16)
    low = jnp.broadcast_to(pos % 16, (R_DEV, HD)).astype(f32).astype(bf16)
    w = GQ * HD
    for d, out in enumerate((q0, q1, q2, q3)):
        h = lax.rem(x + d, N_X)
        out[:, :w] = q_ref[:, pl.ds(pl.multiple_of(h * w, w), w)]
        cols = pl.ds(pl.multiple_of(h * HD, HD), HD)
        out[:, w : w + HD] = rk_ref[:, cols]
        out[:, w + HD : w + 2 * HD] = rv_ref[:, cols]
        out[:, w + 2 * HD : w + 3 * HD] = high
        out[:, w + 3 * HD :] = low


def split_queries(pos, q, rk, rv):
    query = jax.ShapeDtypeStruct((R_DEV, QW), bf16)
    vmem = pl.BlockSpec(memory_space=pltpu.VMEM)
    return pl.pallas_call(
        query_kernel,
        out_shape=(query,) * N_X,
        in_specs=[vmem] * 4,
        out_specs=(vmem,) * N_X,
        name="queries",
    )(pos, q, rk, rv)


def passage_kernel(q_ref, k_ref, v_ref, o_ref):
    ones = jnp.ones((PLEN, HD), bf16)
    values = jnp.concatenate([v_ref[...], ones], axis=1)
    keys = k_ref[...]
    row = lax.broadcasted_iota(jnp.int32, (BLK, BLK), 0)
    col = lax.broadcasted_iota(jnp.int32, (BLK, BLK), 1)
    hidden = jnp.concatenate([col > row] * GQ, axis=0)
    for i in range(NBLK):
        rows = slice(i * BLK, (i + 1) * BLK)
        n = (i + 1) * BLK
        q = jnp.concatenate([q_ref[rows, g * HD : (g + 1) * HD] for g in range(GQ)], axis=0)
        s = lax.dot_general(q, keys[:n], NT, preferred_element_type=f32)
        last = jnp.where(hidden, -jnp.inf, s[:, n - BLK :])
        s = last if i == 0 else jnp.concatenate([s[:, : n - BLK], last], axis=1)
        m = jnp.max(s, axis=1, keepdims=True)
        p = jnp.exp2((s - m) * EXP_SCALE).astype(bf16)
        mixed = jnp.dot(p, values[:n], preferred_element_type=f32)
        out = (mixed[:, :HD] / mixed[:, HD:]).astype(bf16)
        for g in range(GQ):
            o_ref[rows, g * HD : (g + 1) * HD] = out[g * BLK : (g + 1) * BLK]


def encode(q, k, v, first, heads, done):
    w = GQ * HD
    blocks = [
        pl.BlockSpec((PLEN, w), lambda h: (0, first + h)),
        pl.BlockSpec((PLEN, HD), lambda h: (0, first + h)),
        pl.BlockSpec((PLEN, HD), lambda h: (0, first + h)),
    ]
    operands = [q, k, v]
    if done is not None:
        blocks.append(pl.BlockSpec(memory_space=pl.ANY))
        operands.append(done)

    def kernel(q_ref, k_ref, v_ref, *rest):
        passage_kernel(q_ref, k_ref, v_ref, rest[-1])

    return pl.pallas_call(
        kernel,
        out_shape=jax.ShapeDtypeStruct((PLEN, HQ * HD), bf16),
        grid=(heads,),
        in_specs=blocks,
        out_specs=pl.BlockSpec((PLEN, w), lambda h: (0, first + h)),
        input_output_aliases={} if done is None else {3: 0},
        cost_estimate=pl.CostEstimate(
            flops=heads * 4 * PLEN * PLEN * w,
            bytes_accessed=heads * (9 << 18),
            transcendentals=heads * GQ * PLEN * PLEN,
        ),
    )(*operands)


def reader_kernel(half, *refs):
    arrays = 2 * N_Z
    kv_in, refs = refs[:arrays], refs[arrays:]
    q_in, refs = refs[:N_X], refs[N_X:]
    if half:
        mixes, stats = refs[:2]
        outs, refs = refs[2 : 2 + N_X], refs[2 + N_X :]
    else:
        mixes, stats = refs[:2]
        refs = refs[2:]
    kv, keys, values, qs, query, place, olds, scores, top, acc, bases, starts, sems = refs
    x, z, c = place_of()
    copies = [
        pltpu.make_async_copy(kv_in[a], kv.at[pl.ds(N_X * a, N_X)], sems.at[N_X + a]) for a in range(arrays)
    ]
    copies += [
        pltpu.make_async_copy(q_in[d], qs.at[lax.rem(x - d + N_X, N_X)], sems.at[d]) for d in range(N_X)
    ]
    for copy in copies:
        copy.start()
    for copy in copies:
        copy.wait()

    n = jnp.int32(0)
    for t in range(N_SEQ):
        tx, tz, tc = t // (N_Z * 2), (t // 2) % N_Z, t % 2
        piece = lax.rem(c + tc, 2) * 16 + lax.rem(tz - z + N_Z, N_Z) * 4 + lax.rem(x - tx + N_X, N_X)
        count = jnp.max(kv[piece, META : META + 1, :HD].astype(f32)).astype(jnp.int32)
        starts[t] = n
        at = pl.ds(pl.multiple_of(n * ROW, ROW), META)
        keys[at, :] = kv[piece, :META, :HD]
        values[at, :] = kv[piece, :META, HD:]
        for j in range(KEEP):
            bases[n + j] = t * PLEN
        n = n + count
    starts[N_SEQ] = n
    values[pl.ds(pl.multiple_of(n * ROW, ROW), 2 * STEP * ROW), :] = jnp.zeros((2 * STEP * ROW, HD), bf16)
    for j in range(2 * STEP):
        bases[n + j] = FAR * PLEN

    lane = lax.broadcasted_iota(jnp.int32, (1, 2 * ROW), 1)
    w = GQ * HD

    def gather(ref, g):
        return ref[pl.ds(pl.multiple_of(g * STEP * ROW, STEP * ROW), STEP * ROW), :]

    def columns(pair, first, width):
        parts = [qs[2 * pair + r, :, first : first + width] for r in range(2)]
        return jnp.concatenate([parts[r] for r in range(2) for _ in range(GQ)], axis=0)

    def visit(pair, carry):
        shards = [seq_of(2 * pair + r, z, c) for r in range(2)]
        begins = [starts[shards[r]] for r in range(2)]
        ends = [starts[shards[r] + 1] for r in range(2)]
        for r in range(2):
            piece = lax.rem(x - (2 * pair + r) + N_X, N_X)
            for j in range(KEEP):

                @pl.when(begins[r] + j < ends[r])
                def _():
                    number = jnp.max(kv[piece, META + 1 + j : META + 2 + j, :HD].astype(f32)).astype(jnp.int32)
                    bases[begins[r] + j] = shards[r] * PLEN + number * BLK + half * ROW

            for g in range(GQ):
                rows = slice((r * GQ + g) * R_DEV, (r * GQ + g + 1) * R_DEV)
                query[rows, :] = qs[2 * pair + r, :, g * HD : (g + 1) * HD]
        high = columns(pair, w + 2 * HD, HD).astype(f32)
        low = columns(pair, w + 3 * HD, HD).astype(f32)
        row = lax.broadcasted_iota(jnp.int32, (2 * ROWS, 1), 0)
        first = jnp.where(row < ROWS, shards[0] * PLEN, shards[1] * PLEN).astype(f32)
        place[...] = high * 16 + low + first

        if half:
            state = jnp.concatenate([stats[2 * pair + r] for r in range(2)], axis=0)
            old = jnp.broadcast_to(state[:, 0:1], (2 * ROWS, HD))
            olds[...] = old
        else:
            own_k = columns(pair, w, HD).astype(f32)
            own = jnp.sum(query[...].astype(f32) * own_k, axis=1, keepdims=True) * EXP_SCALE
            old = jnp.broadcast_to(own, (2 * ROWS, HD))
            olds[...] = old
        top[...] = old

        def first_pass(g, rows, masked):
            s = lax.dot_general(query[rows, :], gather(keys, g), NT, preferred_element_type=f32)
            best = top[rows, :]
            for u in range(STEP // 2):
                part = s[:, u * HD : (u + 1) * HD] * EXP_SCALE
                if masked:
                    b0 = bases[g * STEP + 2 * u]
                    b1 = bases[g * STEP + 2 * u + 1] - ROW
                    spot = (jnp.where(lane < ROW, b0, b1) + lane).astype(f32)
                    part = jnp.where(spot < place[rows, :], part, -jnp.inf)
                scores[g, rows, u * HD : (u + 1) * HD] = part
                best = jnp.maximum(best, part)
            top[rows, :] = best

        everything, upper = slice(0, 2 * ROWS), slice(ROWS, 2 * ROWS)
        plain = begins[0] // STEP
        both = (ends[0] + STEP - 1) // STEP
        most = (ends[1] + STEP - 1) // STEP

        @pl.loop(0, plain)
        def _(g):
            first_pass(g, everything, False)

        @pl.loop(plain, both)
        def _(g):
            first_pass(g, everything, True)

        @pl.loop(both, most)
        def _(g):
            first_pass(g, upper, True)

        m = jnp.max(top[...], axis=1, keepdims=True)
        wide = jnp.broadcast_to(m, (2 * ROWS, HD))
        top[...] = wide
        if half:
            alpha = jnp.exp2(olds[...] - wide)
            mixed = jnp.concatenate([mixes[2 * pair + r] for r in range(2)], axis=0)
            state = jnp.concatenate([stats[2 * pair + r] for r in range(2)], axis=0)
            acc[:, :HD] = mixed * alpha
            acc[:, HD:] = jnp.where(
                lane == 0, alpha * jnp.broadcast_to(state[:, ROW : ROW + 1], (2 * ROWS, HD)), 0.0
            )
        else:
            alpha = jnp.exp2(olds[...] - wide).astype(bf16).astype(f32)
            acc[:, :HD] = alpha * columns(pair, w + HD, HD).astype(f32)
            acc[:, HD:] = jnp.where(lane == 0, alpha, 0.0)

        def second_pass(g, rows):
            ps = []
            total = acc[rows, HD:]
            for u in range(STEP // 2):
                p = jnp.exp2(scores[g, rows, u * HD : (u + 1) * HD] - top[rows, :])
                total = total + p
                ps.append(p.astype(bf16))
            acc[rows, HD:] = total
            p = jnp.concatenate(ps, axis=1)
            acc[rows, :HD] += jnp.dot(p, gather(values, g), preferred_element_type=f32)

        @pl.loop(0, both)
        def _(g):
            second_pass(g, everything)

        @pl.loop(both, most)
        def _(g):
            second_pass(g, upper)

        total = jnp.sum(acc[:, HD:], axis=1, keepdims=True)
        if half:
            out = (acc[:, :HD] / total).astype(bf16)
            for r in range(2):
                d = lax.rem(x - (2 * pair + r) + N_X, N_X)
                for e in range(N_X):

                    @pl.when(d == e)
                    def _():
                        for g in range(GQ):
                            rows = slice((r * GQ + g) * R_DEV, (r * GQ + g + 1) * R_DEV)
                            outs[e][:, g * HD : (g + 1) * HD] = out[rows]

        else:
            for r in range(2):
                rows = slice(r * ROWS, (r + 1) * ROWS)
                mixes[2 * pair + r] = acc[rows, :HD]
                stats[2 * pair + r] = jnp.where(lane < ROW, top[rows, :], total[rows])
        return carry

    lax.fori_loop(0, N_X // 2, visit, 0)


def read(half, kv_arrays, q_arrays, state):
    out = jax.ShapeDtypeStruct((R_DEV, GQ * HD), bf16)
    kept_state = jax.ShapeDtypeStruct((N_X, ROWS, HD), f32)
    arrays = len(kv_arrays)
    hbm = pl.BlockSpec(memory_space=pl.ANY)
    vmem = pl.BlockSpec(memory_space=pltpu.VMEM)
    most = N_SEQ * KEEP
    return pl.pallas_call(
        functools.partial(reader_kernel, half),
        out_shape=(out,) * N_X if half else (kept_state,) * 2,
        in_specs=[hbm] * (arrays + N_X) + [vmem] * len(state),
        out_specs=(vmem,) * (N_X if half else 2),
        scratch_shapes=[
            pltpu.VMEM((PIECES, PIECE, KV2), bf16),
            pltpu.VMEM(((most + 2 * STEP) * ROW, HD), bf16),
            pltpu.VMEM(((most + 2 * STEP) * ROW, HD), bf16),
            pltpu.VMEM((N_X, R_DEV, QW), bf16),
            pltpu.VMEM((2 * ROWS, HD), bf16),
            pltpu.VMEM((2 * ROWS, HD), f32),
            pltpu.VMEM((2 * ROWS, HD), f32),
            pltpu.VMEM((most // STEP, 2 * ROWS, STEP * ROW), f32),
            pltpu.VMEM((2 * ROWS, HD), f32),
            pltpu.VMEM((2 * ROWS, KV2), f32),
            pltpu.SMEM((most + 2 * STEP,), jnp.int32),
            pltpu.SMEM((N_SEQ + 1,), jnp.int32),
            pltpu.SemaphoreType.DMA((N_X + arrays,)),
        ],
        compiler_params=pltpu.CompilerParams(vmem_limit_bytes=44 << 20),
        cost_estimate=pl.CostEstimate(flops=5 << 30, bytes_accessed=8 << 20, transcendentals=6 << 20),
    )(*kv_arrays, *q_arrays, *state)


def around(a, shift):
    return [shift(a, k) for k in (3, 1, 2)]


def whole(
    passage_q,
    passage_k,
    passage_v,
    kept,
    context_map,
    recompute_pos,
    recompute_q,
    recompute_k,
    recompute_v,
):
    y = lax.axis_index("grp")
    x, _, _ = place_of()
    source = context_map[0, 0] // N_SEQ
    rel = (source - y) % N_GRP

    def across_x(own):
        pieces = [lax.dynamic_index_in_dim(own, (x + d) % N_X, 0, keepdims=True) for d in range(N_X)]
        moved = [pieces[0]] + [shift_seq(pieces[d], dx=d) for d in range(1, N_X)]
        return jnp.concatenate(moved, axis=0)

    def choose(offset, own, others):
        up, down, far = others
        return jnp.where(offset == 0, own, jnp.where(offset == 1, up, jnp.where(offset == 2, far, down)))

    def around_z(near):
        up, down, far = around(near, lambda t, k: shift_seq(t, dz=k))
        return [near, up, far, down]

    def swap(t):
        return shift_seq(t, dc=1)

    fence = lax.optimization_barrier
    first = pack(0, kept, passage_k, passage_v)
    near0 = around(first, shift_y)
    second = pack(1, kept, passage_k, passage_v)
    near1 = around(second, shift_y)
    queries = split_queries(recompute_pos, recompute_q[0], recompute_k[0], recompute_v[0])
    q_arrays = [queries[0]] + [shift_seq(queries[d], dx=d) for d in range(1, N_X)]
    passage_out = encode(passage_q, passage_k, passage_v, 0, 2, None)
    rel, passage_out, q_arrays = fence((rel, passage_out, q_arrays))

    here0 = across_x(choose(rel, first, near0))
    passage_out = encode(passage_q, passage_k, passage_v, 2, 1, passage_out)
    here0, passage_out = fence((here0, passage_out))
    mine0 = around_z(here0)
    passage_out = encode(passage_q, passage_k, passage_v, 3, 1, passage_out)
    rel, passage_out = fence((rel, passage_out))
    here1 = across_x(choose(rel, second, near1))
    mine1 = around_z(here1)
    near, up, down = (swap(mine0[e]) for e in (0, 1, 3))
    far = swap(mine0[2])
    kv0 = mine0 + [near, up, far, down]
    state = read(0, kv0, q_arrays, ())
    other1 = [swap(mine1[0])]
    state, other1, far1 = fence((state, other1, mine1[1:]))
    mine1 = mine1[:1] + far1
    kv1 = mine1 + other1 + [swap(t) for t in far1]
    outs = read(1, kv1, q_arrays, state)
    back = [outs[0]] + [shift_seq(outs[d], dx=-d) for d in range(1, N_X)]

    def head(h):
        d = (h - x) % N_X
        return jnp.where(d == 0, back[0], jnp.where(d == 1, back[1], jnp.where(d == 2, back[2], back[3])))

    reader_rows = jnp.concatenate([head(h) for h in range(KVH)], axis=1)
    return (passage_out, reader_rows[None])


def solution(mesh):
    return jax.shard_map(
        whole,
        mesh=mesh,
        in_specs=(
            P(("grp", "seq"), None),
            P(("grp", "seq"), None),
            P(("grp", "seq"), None),
            P(("grp", "seq"), None),
            P("grp", "seq"),
            P("grp", "seq"),
            P("grp", "seq", None),
            P("grp", "seq", None),
            P("grp", "seq", None),
        ),
        out_specs=(P(("grp", "seq"), None), P("grp", "seq", None)),
        check_vma=False,
    )
```

```python
import functools
import math

import jax
import jax.numpy as jnp
from jax import lax
from jax.experimental import pallas as pl
from jax.experimental.pallas import tpu as pltpu
from jax.sharding import PartitionSpec as P


HQ = 32
KVH = 4
GQ = HQ // KVH
HD = 128
PLEN = 512
BLK = 128
KEEP = 3
NBLK = PLEN // BLK
R_DEV = 64
N_GRP = 4
N_X = 4
N_Z = 4
N_SEQ = 32
ROW = BLK // 2
META = KEEP * ROW
PIECE = META + 16
KV2 = 2 * HD
QW = GQ * HD + 4 * HD
ROWS = GQ * R_DEV
EXP_SCALE = HD ** (-0.5) * math.log2(math.e)
FAR = 100
STEP = 16
PIECES = N_SEQ


NT = (((1,), (1,)), ((), ()))
bf16 = jnp.bfloat16
f32 = jnp.float32


def seq_of(x, z, c):
    return x * (N_Z * 2) + z * 2 + c


def shift_y(a, k):
    return lax.ppermute(a, "grp", [(i, (i + k) % N_GRP) for i in range(N_GRP)])


def seq_pairs(dx, dz, dc):
    return [
        (seq_of(x, z, c), seq_of((x + dx) % N_X, (z + dz) % N_Z, (c + dc) % 2))
        for x in range(N_X)
        for z in range(N_Z)
        for c in range(2)
    ]


def shift_seq(a, dx=0, dz=0, dc=0):
    return lax.ppermute(a, "seq", seq_pairs(dx, dz, dc))


def place_of():
    s = lax.axis_index("seq")
    return s // (N_Z * 2), lax.rem(s // 2, N_Z), lax.rem(s, 2)


def pack_kernel(half, kept_ref, k_ref, v_ref, out, k_rows, v_rows, sems):
    kept = [kept_ref[0, b] for b in range(NBLK)]
    before = [0]
    for b in range(NBLK):
        before.append(before[-1] + kept[b])
    count = before[NBLK]
    row = lax.broadcasted_iota(jnp.int32, (16, HD), 0)
    meta = jnp.where(row == 0, count, FAR)
    copies = []
    for j in range(KEEP):
        block = 0
        for b in range(NBLK):
            block = block + jnp.where((kept[b] > 0) & (before[b] == j), b, 0)
        meta = jnp.where(row == 1 + j, jnp.where(j < count, block, FAR), meta)
        start = pl.multiple_of(block * BLK + half * ROW, ROW)
        copies.append(pltpu.make_async_copy(k_ref.at[pl.ds(start, ROW)], k_rows.at[j], sems.at[2 * j]))
        copies.append(pltpu.make_async_copy(v_ref.at[pl.ds(start, ROW)], v_rows.at[j], sems.at[2 * j + 1]))
        copies[-2].start()
        copies[-1].start()
    for copy in copies:
        copy.wait()
    for j in range(KEEP):
        rows = slice(j * ROW, (j + 1) * ROW)
        for h in range(KVH):
            cols = slice(h * HD, (h + 1) * HD)
            out[h, rows, :HD] = k_rows[j, :, cols]
            out[h, rows, HD:] = v_rows[j, :, cols]
    meta = meta.astype(f32).astype(bf16)
    for h in range(KVH):
        out[h, META:, :HD] = meta
        out[h, META:, HD:] = meta


def pack(half, kept, k, v):
    vmem = pl.BlockSpec(memory_space=pltpu.VMEM)
    return pl.pallas_call(
        functools.partial(pack_kernel, half),
        out_shape=jax.ShapeDtypeStruct((KVH, PIECE, KV2), bf16),
        in_specs=[pl.BlockSpec(memory_space=pltpu.SMEM)] + [pl.BlockSpec(memory_space=pl.ANY)] * 2,
        out_specs=vmem,
        scratch_shapes=[
            pltpu.VMEM((KEEP, ROW, KVH * HD), bf16),
            pltpu.VMEM((KEEP, ROW, KVH * HD), bf16),
            pltpu.SemaphoreType.DMA((2 * KEEP,)),
        ],
        compiler_params=pltpu.CompilerParams(vmem_limit_bytes=60 << 20),
    )(kept, k, v)


def query_kernel(pos_ref, q_ref, rk_ref, rv_ref, q0, q1, q2, q3):
    x, z, c = place_of()
    row = lax.broadcasted_iota(jnp.int32, (R_DEV, R_DEV), 0)
    col = lax.broadcasted_iota(jnp.int32, (R_DEV, R_DEV), 1)
    pos = (pos_ref[...] - seq_of(x, z, c) * PLEN).astype(f32)
    pos = jnp.sum(jnp.where(row == col, pos, 0.0), axis=1, keepdims=True).astype(jnp.int32)
    high = jnp.broadcast_to(pos // 16, (R_DEV, HD)).astype(f32).astype(bf16)
    low = jnp.broadcast_to(pos % 16, (R_DEV, HD)).astype(f32).astype(bf16)
    w = GQ * HD
    for d, out in enumerate((q0, q1, q2, q3)):
        h = lax.rem(x + d, N_X)
        out[:, :w] = q_ref[:, pl.ds(pl.multiple_of(h * w, w), w)]
        cols = pl.ds(pl.multiple_of(h * HD, HD), HD)
        out[:, w : w + HD] = rk_ref[:, cols]
        out[:, w + HD : w + 2 * HD] = rv_ref[:, cols]
        out[:, w + 2 * HD : w + 3 * HD] = high
        out[:, w + 3 * HD :] = low


def split_queries(pos, q, rk, rv):
    query = jax.ShapeDtypeStruct((R_DEV, QW), bf16)
    vmem = pl.BlockSpec(memory_space=pltpu.VMEM)
    return pl.pallas_call(
        query_kernel,
        out_shape=(query,) * N_X,
        in_specs=[vmem] * 4,
        out_specs=(vmem,) * N_X,
        name="queries",
    )(pos, q, rk, rv)


def passage_kernel(q_ref, k_ref, v_ref, o_ref):
    ones = jnp.ones((PLEN, HD), bf16)
    values = jnp.concatenate([v_ref[...], ones], axis=1)
    keys = k_ref[...]
    row = lax.broadcasted_iota(jnp.int32, (BLK, BLK), 0)
    col = lax.broadcasted_iota(jnp.int32, (BLK, BLK), 1)
    hidden = jnp.concatenate([col > row] * GQ, axis=0)
    for i in range(NBLK):
        rows = slice(i * BLK, (i + 1) * BLK)
        n = (i + 1) * BLK
        q = jnp.concatenate([q_ref[rows, g * HD : (g + 1) * HD] for g in range(GQ)], axis=0)
        s = lax.dot_general(q, keys[:n], NT, preferred_element_type=f32)
        last = jnp.where(hidden, -jnp.inf, s[:, n - BLK :])
        s = last if i == 0 else jnp.concatenate([s[:, : n - BLK], last], axis=1)
        m = jnp.max(s, axis=1, keepdims=True)
        p = jnp.exp2((s - m) * EXP_SCALE).astype(bf16)
        mixed = jnp.dot(p, values[:n], preferred_element_type=f32)
        out = (mixed[:, :HD] / mixed[:, HD:]).astype(bf16)
        for g in range(GQ):
            o_ref[rows, g * HD : (g + 1) * HD] = out[g * BLK : (g + 1) * BLK]


def encode(q, k, v, first, heads, done):
    w = GQ * HD
    blocks = [
        pl.BlockSpec((PLEN, w), lambda h: (0, first + h)),
        pl.BlockSpec((PLEN, HD), lambda h: (0, first + h)),
        pl.BlockSpec((PLEN, HD), lambda h: (0, first + h)),
    ]
    operands = [q, k, v]
    if done is not None:
        blocks.append(pl.BlockSpec(memory_space=pl.ANY))
        operands.append(done)

    def kernel(q_ref, k_ref, v_ref, *rest):
        passage_kernel(q_ref, k_ref, v_ref, rest[-1])

    return pl.pallas_call(
        kernel,
        out_shape=jax.ShapeDtypeStruct((PLEN, HQ * HD), bf16),
        grid=(heads,),
        in_specs=blocks,
        out_specs=pl.BlockSpec((PLEN, w), lambda h: (0, first + h)),
        input_output_aliases={} if done is None else {3: 0},
        cost_estimate=pl.CostEstimate(
            flops=heads * 4 * PLEN * PLEN * w,
            bytes_accessed=heads * (9 << 18),
            transcendentals=heads * GQ * PLEN * PLEN,
        ),
    )(*operands)


def reader_kernel(half, *refs):
    arrays = 2 * N_Z
    kv_in, refs = refs[:arrays], refs[arrays:]
    q_in, refs = refs[:N_X], refs[N_X:]
    if half:
        mixes, stats = refs[:2]
        outs, refs = refs[2 : 2 + N_X], refs[2 + N_X :]
    else:
        mixes, stats = refs[:2]
        refs = refs[2:]
    kv, keys, values, qs, query, place, olds, scores, top, acc, bases, starts, sems = refs
    x, z, c = place_of()
    copies = [
        pltpu.make_async_copy(kv_in[a], kv.at[pl.ds(N_X * a, N_X)], sems.at[N_X + a]) for a in range(arrays)
    ]
    copies += [
        pltpu.make_async_copy(q_in[d], qs.at[lax.rem(x - d + N_X, N_X)], sems.at[d]) for d in range(N_X)
    ]
    for copy in copies:
        copy.start()
    for copy in copies:
        copy.wait()

    n = jnp.int32(0)
    for t in range(N_SEQ):
        tx, tz, tc = t // (N_Z * 2), (t // 2) % N_Z, t % 2
        piece = lax.rem(c + tc, 2) * 16 + lax.rem(tz - z + N_Z, N_Z) * 4 + lax.rem(x - tx + N_X, N_X)
        count = jnp.max(kv[piece, META : META + 1, :HD].astype(f32)).astype(jnp.int32)
        starts[t] = n
        at = pl.ds(pl.multiple_of(n * ROW, ROW), META)
        keys[at, :] = kv[piece, :META, :HD]
        values[at, :] = kv[piece, :META, HD:]
        for j in range(KEEP):
            bases[n + j] = t * PLEN
        n = n + count
    starts[N_SEQ] = n
    values[pl.ds(pl.multiple_of(n * ROW, ROW), 2 * STEP * ROW), :] = jnp.zeros((2 * STEP * ROW, HD), bf16)
    for j in range(2 * STEP):
        bases[n + j] = FAR * PLEN

    lane = lax.broadcasted_iota(jnp.int32, (1, 2 * ROW), 1)
    w = GQ * HD

    def gather(ref, g):
        return ref[pl.ds(pl.multiple_of(g * STEP * ROW, STEP * ROW), STEP * ROW), :]

    def columns(pair, first, width):
        parts = [qs[2 * pair + r, :, first : first + width] for r in range(2)]
        return jnp.concatenate([parts[r] for r in range(2) for _ in range(GQ)], axis=0)

    def visit(pair, carry):
        shards = [seq_of(2 * pair + r, z, c) for r in range(2)]
        begins = [starts[shards[r]] for r in range(2)]
        ends = [starts[shards[r] + 1] for r in range(2)]
        for r in range(2):
            piece = lax.rem(x - (2 * pair + r) + N_X, N_X)
            for j in range(KEEP):

                @pl.when(begins[r] + j < ends[r])
                def _():
                    number = jnp.max(kv[piece, META + 1 + j : META + 2 + j, :HD].astype(f32)).astype(jnp.int32)
                    bases[begins[r] + j] = shards[r] * PLEN + number * BLK + half * ROW

            for g in range(GQ):
                rows = slice((r * GQ + g) * R_DEV, (r * GQ + g + 1) * R_DEV)
                query[rows, :] = qs[2 * pair + r, :, g * HD : (g + 1) * HD]
        high = columns(pair, w + 2 * HD, HD).astype(f32)
        low = columns(pair, w + 3 * HD, HD).astype(f32)
        row = lax.broadcasted_iota(jnp.int32, (2 * ROWS, 1), 0)
        first = jnp.where(row < ROWS, shards[0] * PLEN, shards[1] * PLEN).astype(f32)
        place[...] = high * 16 + low + first

        if half:
            state = jnp.concatenate([stats[2 * pair + r] for r in range(2)], axis=0)
            old = jnp.broadcast_to(state[:, 0:1], (2 * ROWS, HD))
            olds[...] = old
        else:
            own_k = columns(pair, w, HD).astype(f32)
            own = jnp.sum(query[...].astype(f32) * own_k, axis=1, keepdims=True) * EXP_SCALE
            old = jnp.broadcast_to(own, (2 * ROWS, HD))
            olds[...] = old
        top[...] = old

        def first_pass(g, rows, masked):
            s = lax.dot_general(query[rows, :], gather(keys, g), NT, preferred_element_type=f32)
            best = top[rows, :]
            for u in range(STEP // 2):
                part = s[:, u * HD : (u + 1) * HD] * EXP_SCALE
                if masked:
                    b0 = bases[g * STEP + 2 * u]
                    b1 = bases[g * STEP + 2 * u + 1] - ROW
                    spot = (jnp.where(lane < ROW, b0, b1) + lane).astype(f32)
                    part = jnp.where(spot < place[rows, :], part, -jnp.inf)
                scores[g, rows, u * HD : (u + 1) * HD] = part
                best = jnp.maximum(best, part)
            top[rows, :] = best

        everything, upper = slice(0, 2 * ROWS), slice(ROWS, 2 * ROWS)
        plain = begins[0] // STEP
        both = (ends[0] + STEP - 1) // STEP
        most = (ends[1] + STEP - 1) // STEP

        @pl.loop(0, plain)
        def _(g):
            first_pass(g, everything, False)

        @pl.loop(plain, both)
        def _(g):
            first_pass(g, everything, True)

        @pl.loop(both, most)
        def _(g):
            first_pass(g, upper, True)

        m = jnp.max(top[...], axis=1, keepdims=True)
        wide = jnp.broadcast_to(m, (2 * ROWS, HD))
        top[...] = wide
        if half:
            alpha = jnp.exp2(olds[...] - wide)
            mixed = jnp.concatenate([mixes[2 * pair + r] for r in range(2)], axis=0)
            state = jnp.concatenate([stats[2 * pair + r] for r in range(2)], axis=0)
            acc[:, :HD] = mixed * alpha
            acc[:, HD:] = jnp.where(
                lane == 0, alpha * jnp.broadcast_to(state[:, ROW : ROW + 1], (2 * ROWS, HD)), 0.0
            )
        else:
            alpha = jnp.exp2(olds[...] - wide).astype(bf16).astype(f32)
            acc[:, :HD] = alpha * columns(pair, w + HD, HD).astype(f32)
            acc[:, HD:] = jnp.where(lane == 0, alpha, 0.0)

        def second_pass(g, rows):
            ps = []
            total = acc[rows, HD:]
            for u in range(STEP // 2):
                p = jnp.exp2(scores[g, rows, u * HD : (u + 1) * HD] - top[rows, :])
                total = total + p
                ps.append(p.astype(bf16))
            acc[rows, HD:] = total
            p = jnp.concatenate(ps, axis=1)
            acc[rows, :HD] += jnp.dot(p, gather(values, g), preferred_element_type=f32)

        @pl.loop(0, both)
        def _(g):
            second_pass(g, everything)

        @pl.loop(both, most)
        def _(g):
            second_pass(g, upper)

        total = jnp.sum(acc[:, HD:], axis=1, keepdims=True)
        if half:
            out = (acc[:, :HD] / total).astype(bf16)
            for r in range(2):
                d = lax.rem(x - (2 * pair + r) + N_X, N_X)
                for e in range(N_X):

                    @pl.when(d == e)
                    def _():
                        for g in range(GQ):
                            rows = slice((r * GQ + g) * R_DEV, (r * GQ + g + 1) * R_DEV)
                            outs[e][:, g * HD : (g + 1) * HD] = out[rows]

        else:
            for r in range(2):
                rows = slice(r * ROWS, (r + 1) * ROWS)
                mixes[2 * pair + r] = acc[rows, :HD]
                stats[2 * pair + r] = jnp.where(lane < ROW, top[rows, :], total[rows])
        return carry

    lax.fori_loop(0, N_X // 2, visit, 0)


def read(half, kv_arrays, q_arrays, state):
    out = jax.ShapeDtypeStruct((R_DEV, GQ * HD), bf16)
    kept_state = jax.ShapeDtypeStruct((N_X, ROWS, HD), f32)
    arrays = len(kv_arrays)
    hbm = pl.BlockSpec(memory_space=pl.ANY)
    vmem = pl.BlockSpec(memory_space=pltpu.VMEM)
    most = N_SEQ * KEEP
    return pl.pallas_call(
        functools.partial(reader_kernel, half),
        out_shape=(out,) * N_X if half else (kept_state,) * 2,
        in_specs=[hbm] * (arrays + N_X) + [vmem] * len(state),
        out_specs=(vmem,) * (N_X if half else 2),
        scratch_shapes=[
            pltpu.VMEM((PIECES, PIECE, KV2), bf16),
            pltpu.VMEM(((most + 2 * STEP) * ROW, HD), bf16),
            pltpu.VMEM(((most + 2 * STEP) * ROW, HD), bf16),
            pltpu.VMEM((N_X, R_DEV, QW), bf16),
            pltpu.VMEM((2 * ROWS, HD), bf16),
            pltpu.VMEM((2 * ROWS, HD), f32),
            pltpu.VMEM((2 * ROWS, HD), f32),
            pltpu.VMEM((most // STEP, 2 * ROWS, STEP * ROW), f32),
            pltpu.VMEM((2 * ROWS, HD), f32),
            pltpu.VMEM((2 * ROWS, KV2), f32),
            pltpu.SMEM((most + 2 * STEP,), jnp.int32),
            pltpu.SMEM((N_SEQ + 1,), jnp.int32),
            pltpu.SemaphoreType.DMA((N_X + arrays,)),
        ],
        compiler_params=pltpu.CompilerParams(vmem_limit_bytes=44 << 20),
        cost_estimate=pl.CostEstimate(flops=5 << 30, bytes_accessed=8 << 20, transcendentals=6 << 20),
    )(*kv_arrays, *q_arrays, *state)


def around(a, shift):
    return [shift(a, k) for k in (3, 1, 2)]


def whole(
    passage_q,
    passage_k,
    passage_v,
    kept,
    context_map,
    recompute_pos,
    recompute_q,
    recompute_k,
    recompute_v,
):
    y = lax.axis_index("grp")
    x, _, _ = place_of()
    source = context_map[0, 0] // N_SEQ
    rel = (source - y) % N_GRP

    def across_x(own):
        pieces = [lax.dynamic_index_in_dim(own, (x + d) % N_X, 0, keepdims=True) for d in range(N_X)]
        moved = [pieces[0]] + [shift_seq(pieces[d], dx=d) for d in range(1, N_X)]
        return jnp.concatenate(moved, axis=0)

    def choose(offset, own, others):
        up, down, far = others
        return jnp.where(offset == 0, own, jnp.where(offset == 1, up, jnp.where(offset == 2, far, down)))

    def around_z(near):
        up, down, far = around(near, lambda t, k: shift_seq(t, dz=k))
        return [near, up, far, down]

    def swap(t):
        return shift_seq(t, dc=1)

    fence = lax.optimization_barrier
    first = pack(0, kept, passage_k, passage_v)
    near0 = around(first, shift_y)
    second = pack(1, kept, passage_k, passage_v)
    near1 = around(second, shift_y)
    queries = split_queries(recompute_pos, recompute_q[0], recompute_k[0], recompute_v[0])
    q_arrays = [queries[0]] + [shift_seq(queries[d], dx=d) for d in range(1, N_X)]
    passage_out = encode(passage_q, passage_k, passage_v, 0, 2, None)
    rel, passage_out, q_arrays = fence((rel, passage_out, q_arrays))

    here0 = across_x(choose(rel, first, near0))
    passage_out = encode(passage_q, passage_k, passage_v, 2, 1, passage_out)
    here0, passage_out = fence((here0, passage_out))
    mine0 = around_z(here0)
    passage_out = encode(passage_q, passage_k, passage_v, 3, 1, passage_out)
    rel, passage_out = fence((rel, passage_out))
    here1 = across_x(choose(rel, second, near1))
    mine1 = around_z(here1)
    near, up, down = (swap(mine0[e]) for e in (0, 1, 3))
    far = swap(mine0[2])
    kv0 = mine0 + [near, up, far, down]
    state = read(0, kv0, q_arrays, ())
    other1 = [swap(mine1[0])]
    state, other1, far1 = fence((state, other1, mine1[1:]))
    mine1 = mine1[:1] + far1
    kv1 = mine1 + other1 + [swap(t) for t in far1]
    outs = read(1, kv1, q_arrays, state)
    back = [outs[0]] + [shift_seq(outs[d], dx=-d) for d in range(1, N_X)]

    def head(h):
        d = (h - x) % N_X
        return jnp.where(d == 0, back[0], jnp.where(d == 1, back[1], jnp.where(d == 2, back[2], back[3])))

    reader_rows = jnp.concatenate([head(h) for h in range(KVH)], axis=1)
    return (passage_out, reader_rows[None])


def solution(mesh):
    return jax.shard_map(
        whole,
        mesh=mesh,
        in_specs=(
            P(("grp", "seq"), None),
            P(("grp", "seq"), None),
            P(("grp", "seq"), None),
            P(("grp", "seq"), None),
            P("grp", "seq"),
            P("grp", "seq"),
            P("grp", "seq", None),
            P("grp", "seq", None),
            P("grp", "seq", None),
        ),
        out_specs=(P(("grp", "seq"), None), P("grp", "seq", None)),
        check_vma=False,
    )
```
